128 devices in a mesh: col: 8 (over x, z_lo), row: 16 (over y, z_hi, core).
Axes of the slice: x: 4, y: 4, z: 4 (z_hi: 2, z_lo: 2; z = z_hi * 2 + z_lo), core: 2. Of those that a mesh axis runs over, the one named last changes fastest.
Arguments:
- covariance: float32 [12288, 12288], P('row', 'col'), may hold values from -2 to 2, as said below
- wfs_map: int32 [12288], P('row'), may hold values from 0 to 5
- noise_var: float32 [6], replicated, may hold values from 0.5 to 2
- targets: float32 [12288, 2048], P('row', 'col'), may hold values from -0.6 to 0.6
- target_pos: float32 [2, 2048], replicated, may hold values from -1 to 1
- layer_strength: float32 [35], replicated, may hold values from 0.005 to 0.05
- layer_scale: float32 [35], replicated, may hold values from 0.2 to 2
- tile_layer: int32 [16], replicated, may hold values from 0 to 34
Outputs:
- updated: float32 [12288, 12288], P('row', 'col')
- panel_factor: float32 [12288, 256], P('row')
- reconstructor: float32 [12288, 2048], P('row', 'col')
- error_cov: float32 [2048, 2048], P('row', 'col')
The draws below stay inside these ranges and needn't reach their ends.
Inputs may be any that keep to these rules, and one draw needn't show every extreme that they name: `covariance`: symmetric and positive semidefinite; its diagonal lies between 0.5 and 2.
All inputs are finite; a program needn't handle non-finite values.
Results may differ from the reference program's by a relative error of at most 0.0003.
Values sent between devices are 32-bit elements; how exact they have to be, the bound alone decides.
No kernel may reach another device: no remote copies, remote signals or barrier semaphores. Data moves between devices by JAX's collectives and lax.ppermute only.
A program may use at most 64 MiB of HBM per device.

```python
import math
import jax
import jax.numpy as jnp
from jax import lax

M = 12288
PB = 256
TC = 2048
TILE = 128
NL = 35
NWFS = 6


def draw_covariance(key, part):
    key_base = jax.random.fold_in(key, 11)
    indices = jnp.arange(M, dtype=jnp.int32)
    base_draw = jax.random.normal(key_base, (M, PB), jnp.float32)
    row_scale = jnp.ones((M,), jnp.float32)
    smooth = base_draw
    weight = 1.0
    for lag in range(1, 8):
        weight = weight * 0.8
        smooth = smooth + weight * jnp.roll(base_draw, lag, axis=0)
    gram = jnp.dot(smooth, smooth.T, precision=lax.Precision.HIGHEST)
    norms = jnp.sum(smooth * smooth, axis=1)
    inverse = row_scale / jnp.sqrt(norms)
    gram = gram * inverse[:, None] * inverse[None, :]
    symmetric = jnp.where(indices[:, None] >= indices[None, :], gram, gram.T)
    symmetric = jnp.clip(symmetric, -2.0, 2.0)
    return symmetric.at[indices, indices].set(row_scale)


def place_ends(entries, stream_key, smallest, high):
    extent = entries.shape
    spot = [jax.random.randint(jax.random.fold_in(stream_key, axis), (), 0, extent[axis]) for axis in range(len(extent))]
    entries = entries.at[tuple(spot)].set(smallest)
    longest = extent.index(max(extent))
    spot[longest] = (spot[longest] + 1) % extent[longest]
    return entries.at[tuple(spot)].set(high)


def steps_of(key, shape, split, smallest, high):
    factor_of = 1.0
    for dim, blocks in split:
        steps = jax.random.uniform(jax.random.fold_in(jax.random.fold_in(key, 6), dim), (blocks,), jnp.float32, smallest / len(split), high / len(split))
        factor_of = factor_of * jnp.repeat(jnp.exp(steps), shape[dim] // blocks).reshape((-1,) + (1,) * (len(shape) - 1 - dim))
    return factor_of


def bell_draw(stream_key, extent, scale, most, pieces=(), kind=jnp.bfloat16):
    result = scale * jax.random.normal(stream_key, extent, jnp.float32)
    if pieces:
        result = result * steps_of(stream_key, extent, pieces, -0.22, 0.18)
    return jnp.clip(result, -most, most).astype(kind)


def setup_inputs(seed: int = 0) -> dict:
    streams_of = jax.random.split(jax.random.key(seed), 9)
    covariance = draw_covariance(jax.random.fold_in(streams_of[8], 71), 0)
    wfs_map = place_ends(jax.random.randint(streams_of[1], (M,), 0, NWFS), jax.random.fold_in(streams_of[1], 1), 0, NWFS - 1).astype(jnp.int32)
    noise_var = jnp.clip(jnp.exp(jax.random.uniform(streams_of[2], (NWFS,), jnp.float32, math.log(0.5), math.log(2.0))), 0.5, 2.0)
    targets = bell_draw(streams_of[3], (M, TC), 0.1, 0.6, ((0, 16), (1, 8)), jnp.float32)
    target_pos = jnp.clip(jax.random.uniform(streams_of[4], (2, TC), jnp.float32, -1.0, 1.0), -1.0, 1.0)
    layer_strength = jnp.clip(jnp.exp(jax.random.uniform(streams_of[5], (NL,), jnp.float32, math.log(0.005), math.log(0.05))), 0.005, 0.05)
    layer_scale = jnp.clip(jnp.exp(jax.random.uniform(streams_of[6], (NL,), jnp.float32, math.log(0.2), math.log(2.0))), 0.2, 2.0)
    tile_layer = place_ends(jax.random.randint(streams_of[7], (TC // TILE,), 0, NL), jax.random.fold_in(streams_of[7], 1), 0, NL - 1).astype(jnp.int32)
    return dict(covariance=covariance, wfs_map=wfs_map, noise_var=noise_var, targets=targets, target_pos=target_pos, layer_strength=layer_strength, layer_scale=layer_scale, tile_layer=tile_layer)


precise = lax.Precision.HIGHEST

def target_covariance(pos_rows, pos_cols, layer_rows, layer_cols, layer_strength, layer_scale):
    distance = (pos_rows[0][:, None] - pos_cols[0][None, :]) ** 2 + (pos_rows[1][:, None] - pos_cols[1][None, :]) ** 2
    lowest = jnp.minimum(layer_rows[:, None], layer_cols[None, :])
    levels = jnp.arange(layer_strength.shape[0], dtype=jnp.int32)
    weights = layer_strength[:, None, None] / (1.0 + distance[None] / (layer_scale * layer_scale)[:, None, None])
    return jnp.sum(jnp.where(levels[:, None, None] <= lowest[None], weights, 0.0), axis=0)

def reference(covariance, wfs_map, noise_var, targets, target_pos, layer_strength, layer_scale, tile_layer):
    indices = jnp.arange(M, dtype=jnp.int32)
    matrix = covariance.at[indices, indices].add(noise_var[wfs_map])
    factor = jnp.linalg.cholesky(matrix[:PB, :PB])
    solved = jax.scipy.linalg.solve_triangular(factor, matrix[:, :PB].T, lower=True).T
    top_rows = jnp.concatenate([factor, jnp.zeros((M - PB, PB), jnp.float32)], axis=0)
    panel_factor = jnp.where(indices[:, None] < PB, top_rows, solved)
    block_rows = M // 16

    def update_block(block):
        start = (block * block_rows).astype(jnp.int32)
        rows_here = lax.dynamic_slice_in_dim(panel_factor, start, block_rows, 0)
        matrix_here = lax.dynamic_slice_in_dim(matrix, start, block_rows, 0)
        row_ids = start + jnp.arange(block_rows, dtype=jnp.int32)
        product = jnp.dot(rows_here, panel_factor.T, precision=precise)
        fill_cols = jnp.concatenate([rows_here, jnp.zeros((block_rows, M - PB), jnp.float32)], axis=1)
        trailing = (row_ids[:, None] >= PB) & (indices[None, :] >= PB)
        return jnp.where(trailing, matrix_here - product, jnp.where(indices[None, :] < PB, fill_cols, 0.0))
    updated = lax.map(update_block, jnp.arange(16, dtype=jnp.int32)).reshape(M, M)
    head_rows = jax.scipy.linalg.solve_triangular(factor, targets[:PB], lower=True)
    head_top = jnp.concatenate([head_rows, jnp.zeros((M - PB, TC), jnp.float32)], axis=0)
    reduced = targets - jnp.dot(panel_factor, head_rows, precision=precise)
    reconstructor = jnp.where(indices[:, None] < PB, head_top, reduced)
    layer_all = jnp.repeat(tile_layer, TILE)

    def covariance_block(block):
        start = (block * TILE).astype(jnp.int32)
        return target_covariance(lax.dynamic_slice_in_dim(target_pos, start, TILE, 1), target_pos, lax.dynamic_slice_in_dim(layer_all, start, TILE, 0), layer_all, layer_strength, layer_scale)
    target_cov = lax.map(covariance_block, jnp.arange(TC // TILE, dtype=jnp.int32)).reshape(TC, TC)
    error_cov = target_cov - jnp.dot(head_rows.T, head_rows, precision=precise)
    return (updated, panel_factor, reconstructor, error_cov)
```

```python
import functools

import jax
import jax.numpy as jnp
from jax import lax
from jax.experimental import pallas as pl
from jax.experimental.pallas import tpu as pltpu
from jax.sharding import PartitionSpec as P

PB = 256
HB = 128
TILE = 128
BOTH = ("col", "row")
precise = lax.Precision.HIGHEST
F32 = jnp.float32


def mm(a, b, dims=((1,), (0,))):
    return lax.dot_general(a, b, (dims, ((), ())), precision=precise, preferred_element_type=F32)


def split(x):
    hi = x.astype(jnp.bfloat16)
    return hi, (x - hi.astype(F32)).astype(jnp.bfloat16)


def mm3(a, b, dims=((1,), (0,))):
    dot = lambda x, y: lax.dot_general(x, y, (dims, ((), ())), preferred_element_type=F32)
    return dot(a[0], b[0]) + (dot(a[0], b[1]) + dot(a[1], b[0]))


def inverse_factor(a_ref, w_ref):
    n = a_ref.shape[0]
    rows = lax.broadcasted_iota(jnp.int32, (n, n), 0)
    lanes = lax.broadcasted_iota(jnp.int32, (n, n), 1)
    groups = rows.reshape(n // 8, 8, n)
    w_ref[...] = jnp.where(rows == lanes, 1.0, 0.0).astype(F32)

    def pick(x, index):
        return jnp.take_along_axis(
            x, jnp.full(x.shape, index, jnp.int32), axis=1, mode="promise_in_bounds"
        )

    def step(it, carry):
        k = it * 4
        a = a_ref[...]
        c = [pick(a, k + t).reshape(n // 8, 8, n) for t in range(4)]
        a = a.reshape(n // 8, 8, n)
        w = w_ref[...].reshape(n // 8, 8, n)
        r = [jnp.broadcast_to(a_ref[pl.ds(k + t, 1), :], (8, n)) for t in range(4)]
        v = [jnp.broadcast_to(w_ref[pl.ds(k + t, 1), :], (8, n)) for t in range(4)]
        g = [[pick(r[t], k + s) for s in range(4)] for t in range(4)]
        inv = []
        for t in range(4):
            inv.append(1.0 / g[t][t])
            for s in range(t + 1, 4):
                m = g[t][s] * inv[t]
                for u in range(s, 4):
                    g[s][u] = g[s][u] - m * g[t][u]
                r[s] = r[s] - m * r[t]
                v[s] = v[s] - m * v[t]
        for t in range(4):
            m = c[t] * inv[t]
            for s in range(t + 1, 4):
                c[s] = c[s] - m * g[t][s]
            m = jnp.where(groups >= k + 4, m, 0.0)
            a = a - m * r[t]
            w = w - m * v[t]
        a_ref[...] = a.reshape(n, n)
        w_ref[...] = w.reshape(n, n)
        for t in range(4):
            d = g[t][t]
            y = lax.rsqrt(d)
            y = y * (1.5 - 0.5 * d * y * y)
            w_ref[pl.ds(k + t, 1), :] = (v[t] * y)[:1]
        return carry

    lax.fori_loop(0, n // 4, step, 0)


def factor_kernel(d_ref, out_ref, a_ref, w1_ref, w2_ref):
    a_ref[...] = d_ref[:HB, :HB]
    inverse_factor(a_ref, w1_ref)
    first = w1_ref[...]
    low = mm(d_ref[HB:, :HB], first, ((1,), (1,)))
    a_ref[...] = d_ref[HB:, HB:] - mm(low, low, ((1,), (1,)))
    inverse_factor(a_ref, w2_ref)
    second = w2_ref[...]
    out_ref[:HB, :] = first
    out_ref[HB:PB, :] = -mm(second, mm(low, first))
    out_ref[PB:, :] = second


def inverse_of_factor(block):
    return pl.pallas_call(
        factor_kernel,
        out_shape=jax.ShapeDtypeStruct((3 * HB, HB), F32),
        scratch_shapes=[pltpu.VMEM((HB, HB), F32)] * 3,
        cost_estimate=pl.CostEstimate(
            flops=200_000_000, transcendentals=0, bytes_accessed=80_000_000
        ),
        name="inverse_factor",
    )(block)


def apply_kernel(
    place_ref, noise_ref, wfs_ref, a_ref, t_ref, own_ref, other_ref, inv_ref, ctt_ref,
    upd_ref, pan_ref, rec_ref, err_ref, lt_ref, u_ref, head_ref,
):
    i = pl.program_id(0)
    row, col = place_ref[0], place_ref[1]
    core = lax.rem(row, 2)
    tile, width = upd_ref.shape
    per = a_ref.shape[1] // 2 // HB

    @pl.when(i == 0)
    def _():
        inv = jnp.concatenate(
            [
                jnp.concatenate([inv_ref[:HB, :], jnp.zeros((HB, HB), F32)], axis=1),
                jnp.concatenate([inv_ref[HB:PB, :], inv_ref[PB:, :]], axis=1),
            ],
            axis=0,
        )
        hi, lo = split(inv)
        lt_ref[0], lt_ref[1] = hi, lo
        half = width // 2
        for ref, at, base in ((own_ref, core, 24), (other_ref, 1 - core, 0)):
            stack = ref[:, base : base + 24, :].reshape(2 * half, HB)
            rows = split(jnp.concatenate([stack[:half], stack[half:]], axis=1))
            u = split(mm3((hi, lo), rows, ((1,), (1,))))
            where = pl.ds(pl.multiple_of(at * half, HB), half)
            u_ref[0, :, where] = u[0]
            u_ref[1, :, where] = u[1]
        mine = own_ref[:, 52:56, :].reshape(PB, HB)
        theirs = other_ref[:, 28:32, :].reshape(PB, HB)
        first = jnp.where(core == 0, mine, theirs)
        last = jnp.where(core == 0, theirs, mine)
        head = mm3((hi, lo), split(jnp.concatenate([first, last], axis=1)))
        head_ref[...] = head
        need = mm3((hi, lo), split(own_ref[:, 48:52, :].reshape(PB, HB)))
        err_ref[...] = ctt_ref[...] - mm3(split(need), split(head), ((0,), (0,)))

    inv = (lt_ref[0], lt_ref[1])
    rows = split(
        jnp.concatenate([panel_rows(own_ref, i, tile, 0), panel_rows(own_ref, i, tile, 1)], axis=1)
    )
    panel = mm3(rows, inv, ((1,), (1,)))
    ids = row * (tile * pl.num_programs(0)) + i * tile + lax.broadcasted_iota(jnp.int32, (tile, PB), 0)
    lane = lax.broadcasted_iota(jnp.int32, (tile, PB), 1)
    panel = jnp.where((ids < PB) & (lane > ids), 0.0, panel)
    pan_ref[...] = panel
    pair = split(panel)
    upd_ref[...] = a_ref[...] - mm3(pair, (u_ref[0], u_ref[1]))
    rec_ref[...] = t_ref[...] - mm3(pair, split(head_ref[...]))

    @pl.when(lax.div(row, 2) == col)
    def _():
        at = pl.multiple_of(core * (width // 2) + i * tile, HB)
        noise = jnp.zeros((1, tile), F32)
        for s in range(noise_ref.shape[0]):
            noise = jnp.where(wfs_ref[...] == s, noise_ref[s], noise)
        eye = lax.broadcasted_iota(jnp.int32, (tile, tile), 0) == lax.broadcasted_iota(
            jnp.int32, (tile, tile), 1
        )
        upd_ref[:, pl.ds(at, tile)] = upd_ref[:, pl.ds(at, tile)] + jnp.where(eye, noise, 0.0)

    @pl.when((row == 0) & (i * tile < PB))
    def _():
        upd_ref[...] = jnp.zeros_like(upd_ref)
        rec_ref[...] = head_ref[pl.ds(pl.multiple_of(i * tile, tile), tile), :]

    @pl.when(col == 0)
    def _():
        upd_ref[:, :PB] = panel


def panel_rows(ref, i, tile, half):
    start = half * 6 + i
    groups = tile // 8
    pieces = []
    for g in range(groups):
        tile_id = start * groups + g
        piece = lax.div(tile_id, 3)
        offset = pl.multiple_of(lax.rem(tile_id, 3) * 8, 8)
        pieces.append(ref[piece, pl.ds(offset, 8), :])
    return jnp.concatenate(pieces, axis=0)


def apply(place, noise_var, wfs, covariance, targets, own, other, inv, ctt):
    rows, width = covariance.shape
    tile = 128
    target_width = targets.shape[1]
    whole = lambda x: pl.BlockSpec(x.shape, lambda i: (0,) * x.ndim, pipeline_mode=pl.Buffered(1))
    smem = pl.BlockSpec(memory_space=pltpu.SMEM)
    return pl.pallas_call(
        apply_kernel,
        grid=(rows // tile,),
        in_specs=[
            smem,
            smem,
            pl.BlockSpec((1, tile), lambda i: (0, i)),
            pl.BlockSpec((tile, width), lambda i: (i, 0)),
            pl.BlockSpec((tile, target_width), lambda i: (i, 0)),
            whole(own),
            whole(other),
            whole(inv),
            whole(ctt),
        ],
        out_specs=[
            pl.BlockSpec((tile, width), lambda i: (i, 0)),
            pl.BlockSpec((tile, PB), lambda i: (i, 0)),
            pl.BlockSpec((tile, target_width), lambda i: (i, 0)),
            pl.BlockSpec(ctt.shape, lambda i: (0, 0)),
        ],
        out_shape=[
            jax.ShapeDtypeStruct((rows, width), F32),
            jax.ShapeDtypeStruct((rows, PB), F32),
            jax.ShapeDtypeStruct((rows, target_width), F32),
            jax.ShapeDtypeStruct(ctt.shape, F32),
        ],
        scratch_shapes=[
            pltpu.VMEM((2, PB, PB), jnp.bfloat16),
            pltpu.VMEM((2, PB, width), jnp.bfloat16),
            pltpu.VMEM((PB, target_width), F32),
        ],
        compiler_params=pltpu.CompilerParams(vmem_limit_bytes=48 << 20),
        cost_estimate=pl.CostEstimate(
            flops=3_300_000_000, transcendentals=0, bytes_accessed=15_000_000
        ),
        name="apply",
    )(place, noise_var, wfs[None, :], covariance, targets, own, other, inv, ctt)


def device(x, z_lo, y, z_hi, core):
    return (x * 2 + z_lo) * 16 + y * 4 + z_hi * 2 + core


def spread(value):
    four, two = range(4), range(2)
    index = lax.axis_index("col") * 16 + lax.axis_index("row")
    value = jnp.where(index == 0, value, 0.0)
    rounds = (
        [[(device(0, 0, 0, 0, 0), device(k, 0, 0, 0, 0))] for k in (2, 1, 3)],
        [[(device(x, 0, 0, 0, 0), device(x, 0, k, 0, 0)) for x in four] for k in (2, 1, 3)],
        [
            [(device(x, 0, y, 0, 0), device(x, lo, y, hi, 0)) for x in four for y in four]
            for lo, hi in ((0, 1), (1, 1), (1, 0))
        ],
        [
            [
                (device(x, lo, y, hi, 0), device(x, lo, y, hi, 1))
                for x in four for y in four for lo in two for hi in two
            ]
        ],
    )
    for perms in rounds:
        value = sum([lax.ppermute(value, BOTH, perm) for perm in perms], value)
    return value


def target_covariance(pos_rows, pos_cols, low, strength, scale):
    distance = (pos_rows[0][:, None] - pos_cols[0][None, :]) ** 2 + (
        pos_rows[1][:, None] - pos_cols[1][None, :]
    ) ** 2
    levels = jnp.arange(strength.shape[0], dtype=jnp.int32)
    weights = strength[:, None, None] / (1.0 + distance[None] / (scale * scale)[:, None, None])
    return jnp.sum(jnp.where(levels[:, None, None] <= low[None, None, :], weights, 0.0), axis=0)


def local(covariance, wfs_map, noise_var, targets, target_pos, strength, scale, tile_layer):
    rows, width = covariance.shape
    target_width = targets.shape[1]
    row, col = lax.axis_index("row"), lax.axis_index("col")
    groups = [[c * 16 + 2 * m + k for c in range(8) for m in range(8)] for k in range(2)]
    exchange = lambda x: lax.all_to_all(
        x, BOTH, 0, 0, axis_index_groups=groups, tiled=True
    )

    noise = jnp.sum(
        jnp.where(
            wfs_map[:, None] == jnp.arange(noise_var.shape[0], dtype=jnp.int32)[None, :],
            noise_var[None, :],
            0.0,
        ),
        axis=1,
    )
    row_ids = row * rows + jnp.arange(rows, dtype=jnp.int32)
    col_ids = col * width + jnp.arange(PB, dtype=jnp.int32)
    panel = covariance[:, :PB] + jnp.where(
        row_ids[:, None] == col_ids[None, :], noise[:, None], 0.0
    )
    inv = inverse_of_factor(panel[:PB, :])

    second = lax.ppermute(targets[:PB, HB:], "row", [(0, 1)])
    half = jnp.where(row == 1, second, targets[:PB, :HB])
    pieces = jnp.concatenate([panel[:, :HB], panel[:, HB:]], axis=0).reshape(64, 24, HB)
    half = jnp.pad(half.reshape(64, 4, HB), ((0, 0), (0, 4), (0, 0)))
    held = exchange(jnp.concatenate([pieces, half], axis=1))
    held_panel = held[:8, :24]
    held_head = held.reshape(8, 8, 32, HB)[:, 0, 24:28]

    shape = lambda n: (8, 8, n, HB)
    over_m = lambda x: jnp.broadcast_to(x[None], shape(x.shape[1]))
    over_c = lambda x: jnp.broadcast_to(x[:, None], shape(x.shape[1]))
    wanted = jnp.concatenate(
        [over_m(held_panel), over_c(held_panel), over_m(held_head), over_c(held_head)], axis=2
    )
    own = exchange(wanted.reshape(64, 56, HB))
    other = lax.ppermute(own[:, 24:], "row", [(i, i ^ 1) for i in range(16)])
    inv = spread(inv)

    start = row * TILE
    pos_rows = lax.dynamic_slice_in_dim(target_pos, start, TILE, 1)
    pos_cols = lax.dynamic_slice_in_dim(target_pos, col * target_width, target_width, 1)
    level_cols = lax.dynamic_slice_in_dim(tile_layer, col * (target_width // TILE), target_width // TILE, 0)
    level_row = lax.dynamic_slice_in_dim(tile_layer, row, 1, 0)
    low = jnp.repeat(jnp.minimum(level_row, level_cols), TILE)
    ctt = target_covariance(pos_rows, pos_cols, low, strength, scale)

    place = jnp.stack([row, col]).astype(jnp.int32)
    updated, panel, reconstructor, error = apply(
        place, noise_var, wfs_map, covariance, targets, own, other, inv, ctt
    )
    return updated, panel, reconstructor, error


def solution(mesh):
    placed = (P("row", "col"), P("row"), P(), P("row", "col"), P(), P(), P(), P())
    return jax.shard_map(
        local,
        mesh=mesh,
        in_specs=placed,
        out_specs=(P("row", "col"), P("row", None), P("row", "col"), P("row", "col")),
        check_vma=False,
    )
```

```python
import functools

import jax
import jax.numpy as jnp
from jax import lax
from jax.experimental import pallas as pl
from jax.experimental.pallas import tpu as pltpu
from jax.sharding import PartitionSpec as P

PB = 256
HB = 128
TILE = 128
BOTH = ("col", "row")
precise = lax.Precision.HIGHEST
F32 = jnp.float32


def mm(a, b, dims=((1,), (0,))):
    return lax.dot_general(a, b, (dims, ((), ())), precision=precise, preferred_element_type=F32)


def split(x):
    hi = x.astype(jnp.bfloat16)
    return hi, (x - hi.astype(F32)).astype(jnp.bfloat16)


def mm3(a, b, dims=((1,), (0,))):
    dot = lambda x, y: lax.dot_general(x, y, (dims, ((), ())), preferred_element_type=F32)
    return dot(a[0], b[0]) + (dot(a[0], b[1]) + dot(a[1], b[0]))


def inverse_factor(a_ref, w_ref):
    n = a_ref.shape[0]
    rows = lax.broadcasted_iota(jnp.int32, (n, n), 0)
    lanes = lax.broadcasted_iota(jnp.int32, (n, n), 1)
    groups = rows.reshape(n // 8, 8, n)
    w_ref[...] = jnp.where(rows == lanes, 1.0, 0.0).astype(F32)

    def pick(x, index):
        return jnp.take_along_axis(
            x, jnp.full(x.shape, index, jnp.int32), axis=1, mode="promise_in_bounds"
        )

    def step(it, carry):
        k = it * 4
        a = a_ref[...]
        c = [pick(a, k + t).reshape(n // 8, 8, n) for t in range(4)]
        a = a.reshape(n // 8, 8, n)
        w = w_ref[...].reshape(n // 8, 8, n)
        r = [jnp.broadcast_to(a_ref[pl.ds(k + t, 1), :], (8, n)) for t in range(4)]
        v = [jnp.broadcast_to(w_ref[pl.ds(k + t, 1), :], (8, n)) for t in range(4)]
        g = [[pick(r[t], k + s) for s in range(4)] for t in range(4)]
        inv = []
        for t in range(4):
            inv.append(1.0 / g[t][t])
            for s in range(t + 1, 4):
                m = g[t][s] * inv[t]
                for u in range(s, 4):
                    g[s][u] = g[s][u] - m * g[t][u]
                r[s] = r[s] - m * r[t]
                v[s] = v[s] - m * v[t]
        for t in range(4):
            m = c[t] * inv[t]
            for s in range(t + 1, 4):
                c[s] = c[s] - m * g[t][s]
            m = jnp.where(groups >= k + 4, m, 0.0)
            a = a - m * r[t]
            w = w - m * v[t]
        a_ref[...] = a.reshape(n, n)
        w_ref[...] = w.reshape(n, n)
        for t in range(4):
            d = g[t][t]
            y = lax.rsqrt(d)
            y = y * (1.5 - 0.5 * d * y * y)
            w_ref[pl.ds(k + t, 1), :] = (v[t] * y)[:1]
        return carry

    lax.fori_loop(0, n // 4, step, 0)


def factor_kernel(d_ref, out_ref, a_ref, w1_ref, w2_ref):
    a_ref[...] = d_ref[:HB, :HB]
    inverse_factor(a_ref, w1_ref)
    first = w1_ref[...]
    low = mm(d_ref[HB:, :HB], first, ((1,), (1,)))
    a_ref[...] = d_ref[HB:, HB:] - mm(low, low, ((1,), (1,)))
    inverse_factor(a_ref, w2_ref)
    second = w2_ref[...]
    out_ref[:HB, :] = first
    out_ref[HB:PB, :] = -mm(second, mm(low, first))
    out_ref[PB:, :] = second


def inverse_of_factor(block):
    return pl.pallas_call(
        factor_kernel,
        out_shape=jax.ShapeDtypeStruct((3 * HB, HB), F32),
        scratch_shapes=[pltpu.VMEM((HB, HB), F32)] * 3,
        cost_estimate=pl.CostEstimate(
            flops=200_000_000, transcendentals=0, bytes_accessed=80_000_000
        ),
        name="inverse_factor",
    )(block)


def inverse_pair(inv_ref):
    return split(
        jnp.concatenate(
            [
                jnp.concatenate([inv_ref[:HB, :], jnp.zeros((HB, HB), F32)], axis=1),
                jnp.concatenate([inv_ref[HB:PB, :], inv_ref[PB:, :]], axis=1),
            ],
            axis=0,
        )
    )


def solve_kernel(
    row_ref, noise_ref, own_ref, head_ref, need_ref, inv_ref, ctt_ref,
    pan_ref, lead_ref, err_ref,
):
    inv = inverse_pair(inv_ref)
    pan_ref[...] = mm3(split(own_ref[...]), inv, ((1,), (1,)))

    @pl.when(row_ref[0] == 0)
    def _():
        sub = lax.broadcasted_iota(jnp.int32, (PB, PB), 0)
        lane = lax.broadcasted_iota(jnp.int32, (PB, PB), 1)
        block = own_ref[:PB] + jnp.where(sub == lane, noise_ref[:, :PB], 0.0)
        lead = mm3(split(block), inv, ((1,), (1,)))
        pan_ref[:PB, :] = jnp.where(lane > sub, 0.0, lead)

    head = mm3(inv, split(head_ref[...]))
    need = mm3(inv, split(need_ref[...]))
    lead_ref[...] = head
    err_ref[...] = ctt_ref[...] - mm3(split(need), split(head), ((0,), (0,)))


def columns_kernel(rows_ref, inv_ref, u_ref):
    u_ref[0], u_ref[1] = split(mm3(inverse_pair(inv_ref), split(rows_ref[...]), ((1,), (1,))))


def update_kernel(
    place_ref, noise_ref, a_ref, t_ref, pan_ref, mine_ref, other_ref, head_ref, inv_ref,
    upd_ref, rec_ref, u_ref, pair_ref,
):
    i = pl.program_id(0)
    row, col = place_ref[0], place_ref[1]
    core = lax.rem(row, 2)
    tile, width = upd_ref.shape
    half = width // 2

    @pl.when(i == 0)
    def _():
        u = split(mm3(inverse_pair(inv_ref), split(other_ref[...]), ((1,), (1,))))
        theirs = pl.ds(pl.multiple_of((1 - core) * half, HB), half)
        ours = pl.ds(pl.multiple_of(core * half, HB), half)
        for part in range(2):
            u_ref[part, :, theirs] = u[part]
            u_ref[part, :, ours] = mine_ref[part]
        pair_ref[0], pair_ref[1] = split(head_ref[...])

    pair = split(pan_ref[...])
    here = pl.ds(pl.multiple_of(i * tile, tile), tile)
    upd_ref[...] = a_ref[...] - mm3(pair, (u_ref[0], u_ref[1]))
    rec_ref[...] = t_ref[...] - mm3(pair, (pair_ref[0], pair_ref[1]))

    @pl.when(lax.div(row, 2) == col)
    def _():
        block = pl.ds(pl.multiple_of(core * half + i * tile, HB), tile)
        eye = lax.broadcasted_iota(jnp.int32, (tile, tile), 0) == lax.broadcasted_iota(
            jnp.int32, (tile, tile), 1
        )
        upd_ref[:, block] = upd_ref[:, block] + jnp.where(eye, noise_ref[...], 0.0)

    @pl.when((row == 0) & (i * tile < PB))
    def _():
        upd_ref[...] = jnp.zeros_like(upd_ref)
        rec_ref[...] = head_ref[here, :]

    @pl.when(col == 0)
    def _():
        upd_ref[:, :PB] = pan_ref[...]


SMEM = pl.BlockSpec(memory_space=pltpu.SMEM)
VMEM = pl.BlockSpec(memory_space=pltpu.VMEM)


def solve(place, noise, own, head, need, inv, ctt):
    return pl.pallas_call(
        solve_kernel,
        in_specs=[SMEM] + [VMEM] * 6,
        out_specs=[VMEM] * 3,
        out_shape=[jax.ShapeDtypeStruct(x.shape, F32) for x in (own, head, ctt)],
        cost_estimate=pl.CostEstimate(
            flops=600_000_000, transcendentals=0, bytes_accessed=3_000_000
        ),
        name="solve",
    )(place, noise[None, :], own, head, need, inv, ctt)


def solve_columns(rows, inv):
    return pl.pallas_call(
        columns_kernel,
        in_specs=[VMEM] * 2,
        out_specs=VMEM,
        out_shape=jax.ShapeDtypeStruct((2, PB, rows.shape[0]), jnp.bfloat16),
        cost_estimate=pl.CostEstimate(
            flops=300_000_000, transcendentals=0, bytes_accessed=2_000_000
        ),
        name="solve_columns",
    )(rows, inv)


def update(place, noise, covariance, targets, panel, mine, other, head, inv):
    rows, width = covariance.shape
    tile = 128
    target_width = targets.shape[1]
    tiled = lambda n: pl.BlockSpec((tile, n), lambda i: (i, 0))
    return pl.pallas_call(
        update_kernel,
        grid=(rows // tile,),
        in_specs=[
            SMEM, pl.BlockSpec((1, tile), lambda i: (0, i)), tiled(width), tiled(target_width),
            tiled(PB), VMEM, VMEM, VMEM, VMEM,
        ],
        out_specs=[tiled(width), tiled(target_width)],
        out_shape=[
            jax.ShapeDtypeStruct((rows, width), F32),
            jax.ShapeDtypeStruct((rows, target_width), F32),
        ],
        scratch_shapes=[
            pltpu.VMEM((2, PB, width), jnp.bfloat16),
            pltpu.VMEM((2, PB, target_width), jnp.bfloat16),
        ],
        compiler_params=pltpu.CompilerParams(vmem_limit_bytes=32 << 20),
        cost_estimate=pl.CostEstimate(
            flops=3_000_000_000, transcendentals=0, bytes_accessed=12_000_000
        ),
        name="update",
    )(
        place,
        noise[None, :],
        pltpu.with_memory_space_constraint(covariance, pltpu.HBM),
        pltpu.with_memory_space_constraint(targets, pltpu.HBM),
        panel, mine, other, head, inv,
    )


def device(x, z_lo, y, z_hi, core):
    return (x * 2 + z_lo) * 16 + y * 4 + z_hi * 2 + core


def spread(value):
    four, two = range(4), range(2)
    index = lax.axis_index("col") * 16 + lax.axis_index("row")
    value = jnp.where(index == 0, value, 0.0)
    rounds = (
        [[(device(0, 0, 0, 0, 0), device(k, 0, 0, 0, 0))] for k in (2, 1, 3)],
        [[(device(x, 0, 0, 0, 0), device(x, 0, k, 0, 0)) for x in four] for k in (2, 1, 3)],
        [
            [(device(x, 0, y, 0, 0), device(x, lo, y, hi, 0)) for x in four for y in four]
            for lo, hi in ((0, 1), (1, 1), (1, 0))
        ],
        [
            [
                (device(x, lo, y, hi, 0), device(x, lo, y, hi, 1))
                for x in four for y in four for lo in two for hi in two
            ]
        ],
    )
    values = []
    for perms in rounds:
        value = sum([lax.ppermute(value, BOTH, perm) for perm in perms], value)
        values.append(value)
    return values


def target_covariance(pos_rows, pos_cols, low, strength, scale):
    distance = (pos_rows[0][:, None] - pos_cols[0][None, :]) ** 2 + (
        pos_rows[1][:, None] - pos_cols[1][None, :]
    ) ** 2
    levels = jnp.arange(strength.shape[0], dtype=jnp.int32)
    weights = strength[:, None, None] / (1.0 + distance[None] / (scale * scale)[:, None, None])
    return jnp.sum(jnp.where(levels[:, None, None] <= low[None, None, :], weights, 0.0), axis=0)


def local(covariance, wfs_map, noise_var, targets, target_pos, strength, scale, tile_layer):
    rows, width = covariance.shape
    target_width = targets.shape[1]
    row, col = lax.axis_index("row"), lax.axis_index("col")
    four, eight, two = range(4), range(8), range(2)
    same_core = [[2 * m + k for m in eight] for k in two]
    swap_places = [
        (c * 16 + 2 * m + k, m * 16 + 2 * c + k) for c in eight for m in eight for k in two
    ]

    panel_in = covariance[:, :PB]
    chunk = lax.all_to_all(panel_in, "col", 0, 0, tiled=True)[: rows // 8]

    noise = jnp.sum(
        jnp.where(
            wfs_map[:, None] == jnp.arange(noise_var.shape[0], dtype=jnp.int32)[None, :],
            noise_var[None, :],
            0.0,
        ),
        axis=1,
    )
    block_ids = jnp.arange(PB, dtype=jnp.int32)
    waves = spread(
        covariance[:PB, :PB]
        + jnp.where(block_ids[:, None] == block_ids[None, :], noise[:PB, None], 0.0)
    )

    own = lax.all_to_all(jnp.tile(chunk, (8, 1)), "col", 0, 0, tiled=True)
    turned = lax.ppermute(chunk, BOTH, swap_places)
    turned, _ = lax.optimization_barrier((turned, own))
    turned = jnp.tile(turned, (8, 1))
    lead, turned = lax.optimization_barrier((waves[-1], turned))
    inv = inverse_of_factor(lead)
    mine = lax.all_to_all(turned, "row", 0, 0, axis_index_groups=same_core, tiled=True)

    head, _ = lax.optimization_barrier((jnp.where(row == 0, targets[:PB], 0.0), waves[2]))
    for perms in (
        [[(0, 4 * y)] for y in (2, 1, 3)],
        [[(4 * y, 4 * y + 2) for y in four]],
        [[(2 * m, 2 * m + 1) for m in eight]],
    ):
        head = sum([lax.ppermute(head, "row", perm) for perm in perms], head)
    need = lax.ppermute(
        jnp.where(lax.rem(row, 2) == 0, head[:, :HB], head[:, HB:]), BOTH, swap_places
    )

    start = row * TILE
    pos_rows = lax.dynamic_slice_in_dim(target_pos, start, TILE, 1)
    pos_cols = lax.dynamic_slice_in_dim(target_pos, col * target_width, target_width, 1)
    level_cols = lax.dynamic_slice_in_dim(tile_layer, col * (target_width // TILE), target_width // TILE, 0)
    level_row = lax.dynamic_slice_in_dim(tile_layer, row, 1, 0)
    low = jnp.repeat(jnp.minimum(level_row, level_cols), TILE)
    ctt = target_covariance(pos_rows, pos_cols, low, strength, scale)

    place = jnp.stack([row, col]).astype(jnp.int32)
    panel, head, error = solve(place, noise, own, head, need, inv, ctt)
    mine, inv = lax.optimization_barrier((mine, inv))
    other = lax.ppermute(mine, "row", [(i, i ^ 1) for i in range(16)])
    mine = solve_columns(mine, inv)
    updated, reconstructor = update(
        place, noise, covariance, targets, panel, mine, other, head, inv
    )
    return updated, panel, reconstructor, error


def solution(mesh):
    placed = (P("row", "col"), P("row"), P(), P("row", "col"), P(), P(), P(), P())
    return jax.shard_map(
        local,
        mesh=mesh,
        in_specs=placed,
        out_specs=(P("row", "col"), P("row", None), P("row", "col"), P("row", "col")),
        check_vma=False,
    )
```

```python
import functools

import jax
import jax.numpy as jnp
from jax import lax
from jax.experimental import pallas as pl
from jax.experimental.pallas import tpu as pltpu
from jax.sharding import PartitionSpec as P

PB = 256
HB = 128
TILE = 128
BOTH = ("col", "row")
precise = lax.Precision.HIGHEST
F32 = jnp.float32


def mm(a, b, dims=((1,), (0,))):
    return lax.dot_general(a, b, (dims, ((), ())), precision=precise, preferred_element_type=F32)


def split(x):
    hi = x.astype(jnp.bfloat16)
    return hi, (x - hi.astype(F32)).astype(jnp.bfloat16)


def left(x, axis=1):
    hi, lo = split(x)
    return jnp.concatenate([hi, hi, lo], axis=axis)


def right(x, axis=1):
    hi, lo = split(x)
    return jnp.concatenate([hi, lo, hi], axis=axis)


def dot3(a, b, dims=((1,), (0,))):
    return lax.dot_general(a, b, (dims, ((), ())), preferred_element_type=F32)


def inverse_factor(a_ref, w_ref):
    n = a_ref.shape[0]
    rows = lax.broadcasted_iota(jnp.int32, (n, n), 0)
    lanes = lax.broadcasted_iota(jnp.int32, (n, n), 1)
    groups = rows.reshape(n // 8, 8, n)
    w_ref[...] = jnp.where(rows == lanes, 1.0, 0.0).astype(F32)

    def pick(x, index):
        return jnp.take_along_axis(
            x, jnp.full(x.shape, index, jnp.int32), axis=1, mode="promise_in_bounds"
        )

    def step(it, carry):
        k = it * 4
        a = a_ref[...]
        c = [pick(a, k + t).reshape(n // 8, 8, n) for t in range(4)]
        a = a.reshape(n // 8, 8, n)
        w = w_ref[...].reshape(n // 8, 8, n)
        r = [jnp.broadcast_to(a_ref[pl.ds(k + t, 1), :], (8, n)) for t in range(4)]
        v = [jnp.broadcast_to(w_ref[pl.ds(k + t, 1), :], (8, n)) for t in range(4)]
        g = [[pick(r[t], k + s) for s in range(4)] for t in range(4)]
        inv = []
        for t in range(4):
            inv.append(1.0 / g[t][t])
            for s in range(t + 1, 4):
                m = g[t][s] * inv[t]
                for u in range(s, 4):
                    g[s][u] = g[s][u] - m * g[t][u]
                r[s] = r[s] - m * r[t]
                v[s] = v[s] - m * v[t]
        for t in range(4):
            m = c[t] * inv[t]
            for s in range(t + 1, 4):
                c[s] = c[s] - m * g[t][s]
            m = jnp.where(groups >= k + 4, m, 0.0)
            a = a - m * r[t]
            w = w - m * v[t]
        a_ref[...] = a.reshape(n, n)
        w_ref[...] = w.reshape(n, n)
        for t in range(4):
            d = g[t][t]
            y = lax.rsqrt(d)
            y = y * (1.5 - 0.5 * d * y * y)
            w_ref[pl.ds(k + t, 1), :] = (v[t] * y)[:1]
        return carry

    lax.fori_loop(0, n // 4, step, 0)


def factor_kernel(d_ref, out_ref, a_ref, w1_ref, w2_ref):
    a_ref[...] = d_ref[:HB, :HB]
    inverse_factor(a_ref, w1_ref)
    first = w1_ref[...]
    low = mm(d_ref[HB:, :HB], first, ((1,), (1,)))
    a_ref[...] = d_ref[HB:, HB:] - mm(low, low, ((1,), (1,)))
    inverse_factor(a_ref, w2_ref)
    second = w2_ref[...]
    out_ref[:HB, :] = first
    out_ref[HB:PB, :] = -mm(second, mm(low, first))
    out_ref[PB:, :] = second


def inverse_of_factor(block):
    return pl.pallas_call(
        factor_kernel,
        out_shape=jax.ShapeDtypeStruct((3 * HB, HB), F32),
        scratch_shapes=[pltpu.VMEM((HB, HB), F32)] * 3,
        compiler_params=pltpu.CompilerParams(vmem_limit_bytes=8 << 20),
        cost_estimate=pl.CostEstimate(
            flops=200_000_000, transcendentals=0, bytes_accessed=80_000_000
        ),
        name="inverse_factor",
    )(block)


def two_halves(ref, base):
    stack = ref[:, base : base + 24, :].reshape(-1, HB)
    half = stack.shape[0] // 2
    return jnp.concatenate([stack[:half], stack[half:]], axis=1)


def noise_row(noise_ref, wfs):
    noise = jnp.zeros(wfs.shape, F32)
    for s in range(noise_ref.shape[0]):
        noise = jnp.where(wfs == s, noise_ref[s], noise)
    return noise


def iotas():
    shape = (PB, PB)
    return lax.broadcasted_iota(jnp.int32, shape, 0), lax.broadcasted_iota(jnp.int32, shape, 1)


def solve_kernel(
    place_ref, noise_ref, wfs_ref, own_ref, inv_ref, a_ref, t_ref,
    pan_ref, inv3_ref, pair_ref, mine_ref, a_out, t_out, sems,
):
    copies = [
        pltpu.make_async_copy(a_ref, a_out, sems.at[0]),
        pltpu.make_async_copy(t_ref, t_out, sems.at[1]),
    ]
    for copy in copies:
        copy.start()
    inv = jnp.concatenate(
        [
            jnp.concatenate([inv_ref[:HB, :], jnp.zeros((HB, HB), F32)], axis=1),
            jnp.concatenate([inv_ref[HB:PB, :], inv_ref[PB:, :]], axis=1),
        ],
        axis=0,
    )
    inv3_ref[...] = left(inv)
    inv3 = inv3_ref[...]
    pan_ref[...] = dot3(right(two_halves(own_ref, 0)), inv3, ((1,), (1,)))

    @pl.when(place_ref[0] == 0)
    def _():
        sub, lane = iotas()
        noise = noise_row(noise_ref, wfs_ref[:, :PB])
        block = two_halves(own_ref, 0)[:PB] + jnp.where(sub == lane, noise, 0.0)
        lead = dot3(right(block), inv3, ((1,), (1,)))
        pan_ref[:PB, :] = jnp.where(lane > sub, 0.0, lead)

    pair_ref[...] = left(pan_ref[...])
    mine_ref[...] = right(dot3(inv3, right(two_halves(own_ref, 24)), ((1,), (1,))), axis=0)
    for copy in copies:
        copy.wait()


def solve(place, noise_var, wfs, own, inv, covariance, targets):
    rows = covariance.shape[0]
    anywhere = pl.BlockSpec(memory_space=pl.ANY)
    far = lambda x: pltpu.with_memory_space_constraint(x, pltpu.HBM)
    return pl.pallas_call(
        solve_kernel,
        in_specs=[SMEM, SMEM, VMEM, VMEM, VMEM, anywhere, anywhere],
        out_specs=[VMEM] * 6,
        out_shape=[
            pltpu.VMEM((rows, PB), F32),
            pltpu.VMEM((PB, 3 * PB), jnp.bfloat16),
            pltpu.VMEM((rows, 3 * PB), jnp.bfloat16),
            pltpu.VMEM((3 * PB, rows), jnp.bfloat16),
            pltpu.VMEM(covariance.shape, F32),
            pltpu.VMEM(targets.shape, F32),
        ],
        scratch_shapes=[pltpu.SemaphoreType.DMA((2,))],
        compiler_params=pltpu.CompilerParams(vmem_limit_bytes=20 << 20),
        cost_estimate=pl.CostEstimate(
            flops=1_000_000_000, transcendentals=0, bytes_accessed=6_000_000
        ),
        name="solve",
    )(place, noise_var, wfs[None, :], own, inv, far(covariance), far(targets))


def update_kernel(
    place_ref, noise_ref, wfs_ref, a_ref, t_ref, own_ref, other_ref, panel_ref, inv3_ref, pair_ref,
    mine_ref, ctt_ref, upd_ref, pan_ref, rec_ref, err_ref, theirs_ref, head_ref, head3_ref,
):
    i = pl.program_id(0)
    row, col = place_ref[0], place_ref[1]
    core = lax.rem(row, 2)
    tile, width = upd_ref.shape
    half = width // 2

    @pl.when(i == 0)
    def _():
        inv3 = inv3_ref[...]
        raw = right(two_halves(other_ref, 0))
        theirs_ref[...] = right(dot3(inv3, raw, ((1,), (1,))), axis=0)
        mine = own_ref[:, 52:56, :].reshape(PB, HB)
        other = other_ref[:, 28:32, :].reshape(PB, HB)
        first = jnp.where(core == 0, mine, other)
        last = jnp.where(core == 0, other, mine)
        head = dot3(inv3, right(jnp.concatenate([first, last], axis=1), axis=0))
        head_ref[...] = head
        head3_ref[...] = right(head, axis=0)
        need = dot3(inv3, right(own_ref[:, 48:52, :].reshape(PB, HB), axis=0))
        err_ref[...] = ctt_ref[...] - dot3(left(need, axis=0), head3_ref[...], ((0,), (0,)))

    here = pl.ds(pl.multiple_of(i * tile, tile), tile)
    pair = pair_ref[here, :]
    for at, ref in ((core, mine_ref), (1 - core, theirs_ref)):
        where = pl.ds(pl.multiple_of(at * half, half), half)
        upd_ref[:, where] = a_ref[here, where] - dot3(pair, ref[...])
    pan_ref[...] = panel_ref[here, :]
    rec_ref[...] = t_ref[here, :] - dot3(pair, head3_ref[...])

    @pl.when(lax.div(row, 2) == col)
    def _():
        where = pl.ds(pl.multiple_of(core * half + i * tile, PB), PB)
        sub, lane = iotas()
        noise = noise_row(noise_ref, wfs_ref[...])
        upd_ref[:, where] = upd_ref[:, where] + jnp.where(sub == lane, noise, 0.0)

    @pl.when((row == 0) & (i == 0))
    def _():
        upd_ref[...] = jnp.zeros_like(upd_ref)
        rec_ref[...] = head_ref[...]

    @pl.when(col == 0)
    def _():
        upd_ref[:, :PB] = panel_ref[here, :]


SMEM = pl.BlockSpec(memory_space=pltpu.SMEM)
VMEM = pl.BlockSpec(memory_space=pltpu.VMEM)


def update(place, noise_var, wfs, matrix, targets, own, other, solved, ctt):
    rows, width = matrix.shape
    target_width = targets.shape[1]
    tiled = lambda n: pl.BlockSpec((PB, n), lambda i: (i, 0))
    near = lambda x: pltpu.with_memory_space_constraint(x, pltpu.VMEM)
    return pl.pallas_call(
        update_kernel,
        grid=(rows // PB,),
        in_specs=[SMEM, SMEM, pl.BlockSpec((1, PB), lambda i: (0, i))]
        + [VMEM] * 9,
        out_specs=[
            tiled(width),
            tiled(PB),
            tiled(target_width),
            pl.BlockSpec(ctt.shape, lambda i: (0, 0)),
        ],
        out_shape=[
            jax.ShapeDtypeStruct((rows, width), F32),
            jax.ShapeDtypeStruct((rows, PB), F32),
            jax.ShapeDtypeStruct((rows, target_width), F32),
            jax.ShapeDtypeStruct(ctt.shape, F32),
        ],
        scratch_shapes=[
            pltpu.VMEM((3 * PB, width // 2), jnp.bfloat16),
            pltpu.VMEM((PB, target_width), F32),
            pltpu.VMEM((3 * PB, target_width), jnp.bfloat16),
        ],
        compiler_params=pltpu.CompilerParams(vmem_limit_bytes=20 << 20),
        cost_estimate=pl.CostEstimate(
            flops=2_000_000_000, transcendentals=0, bytes_accessed=7_000_000
        ),
        name="update",
    )(
        place, noise_var, wfs[None, :], near(matrix), near(targets), near(own), near(other),
        *[near(x) for x in solved], near(ctt),
    )


def device(x, z_lo, y, z_hi, core):
    return (x * 2 + z_lo) * 16 + y * 4 + z_hi * 2 + core


def spread(value, first):
    four, two = range(4), range(2)
    index = lax.axis_index("col") * 16 + lax.axis_index("row")
    value = jnp.where(index == 0, value, 0.0)
    rounds = (
        [[(device(0, 0, 0, 0, 0), device(k, 0, 0, 0, 0))] for k in (2, 1, 3)],
        [[(device(x, 0, 0, 0, 0), device(x, 0, k, 0, 0)) for x in four] for k in (2, 1, 3)],
        [
            [(device(x, 0, y, 0, 0), device(x, lo, y, hi, 0)) for x in four for y in four]
            for lo, hi in ((0, 1), (1, 1), (1, 0))
        ],
        [
            [
                (device(x, lo, y, hi, 0), device(x, lo, y, hi, 1))
                for x in four for y in four for lo in two for hi in two
            ]
        ],
    )
    waves = []
    for perms in rounds:
        parts = [lax.ppermute(value, BOTH, perm) for perm in perms]
        value = sum(parts, value)
        if not waves:
            value, _ = lax.optimization_barrier((value, first))
        waves.append(value)
    return waves


def target_covariance(pos_rows, pos_cols, low, strength, scale):
    distance = (pos_rows[0][:, None] - pos_cols[0][None, :]) ** 2 + (
        pos_rows[1][:, None] - pos_cols[1][None, :]
    ) ** 2
    levels = jnp.arange(strength.shape[0], dtype=jnp.int32)
    weights = strength[:, None, None] / (1.0 + distance[None] / (scale * scale)[:, None, None])
    return jnp.sum(jnp.where(levels[:, None, None] <= low[None, None, :], weights, 0.0), axis=0)


def local(covariance, wfs_map, noise_var, targets, target_pos, strength, scale, tile_layer):
    rows, width = covariance.shape
    target_width = targets.shape[1]
    row, col = lax.axis_index("row"), lax.axis_index("col")
    groups = [[c * 16 + 2 * m + k for c in range(8) for m in range(8)] for k in range(2)]
    exchange = lambda x: lax.all_to_all(
        x, BOTH, 0, 0, axis_index_groups=groups, tiled=True
    )

    second = lax.ppermute(targets[:PB, HB:], "row", [(0, 1)])
    half = jnp.where(row == 1, second, targets[:PB, :HB])
    half = jnp.pad(half.reshape(64, 4, HB), ((0, 0), (0, 4), (0, 0)))
    pieces = jnp.concatenate([covariance[:, :HB], covariance[:, HB:PB]], axis=0)
    pieces = jnp.concatenate([pieces.reshape(64, 24, HB), half], axis=1)

    noise = jnp.sum(
        jnp.where(
            wfs_map[:PB, None] == jnp.arange(noise_var.shape[0], dtype=jnp.int32)[None, :],
            noise_var[None, :],
            0.0,
        ),
        axis=1,
    )
    ids = jnp.arange(PB, dtype=jnp.int32)
    waves = spread(
        covariance[:PB, :PB] + jnp.where(ids[:, None] == ids[None, :], noise[:, None], 0.0),
        pieces,
    )
    held = exchange(pieces)
    held, _ = lax.optimization_barrier((held, waves[2]))
    held_panel = held[:8, :24]
    held_head = held.reshape(8, 8, 32, HB)[:, 0, 24:28]

    shape = lambda n: (8, 8, n, HB)
    over_m = lambda x: jnp.broadcast_to(x[None], shape(x.shape[1]))
    over_c = lambda x: jnp.broadcast_to(x[:, None], shape(x.shape[1]))
    wanted = jnp.concatenate(
        [over_m(held_panel), over_c(held_panel), over_m(held_head), over_c(held_head)], axis=2
    ).reshape(64, 56, HB)
    lead, _ = lax.optimization_barrier((waves[-1], wanted))
    inv = inverse_of_factor(lead)
    own, inv = lax.optimization_barrier((exchange(wanted), inv))
    other = lax.ppermute(own[:, 24:], "row", [(i, i ^ 1) for i in range(16)])

    start = row * TILE
    pos_rows = lax.dynamic_slice_in_dim(target_pos, start, TILE, 1)
    pos_cols = lax.dynamic_slice_in_dim(target_pos, col * target_width, target_width, 1)
    level_cols = lax.dynamic_slice_in_dim(tile_layer, col * (target_width // TILE), target_width // TILE, 0)
    level_row = lax.dynamic_slice_in_dim(tile_layer, row, 1, 0)
    low = jnp.repeat(jnp.minimum(level_row, level_cols), TILE)
    ctt = target_covariance(pos_rows, pos_cols, low, strength, scale)

    place = jnp.stack([row, col]).astype(jnp.int32)
    *solved, matrix, near_targets = solve(
        place, noise_var, wfs_map, own, inv, covariance, targets
    )
    return update(
        place, noise_var, wfs_map, matrix, near_targets, own, other, solved, ctt
    )


def solution(mesh):
    placed = (P("row", "col"), P("row"), P(), P("row", "col"), P(), P(), P(), P())
    return jax.shard_map(
        local,
        mesh=mesh,
        in_specs=placed,
        out_specs=(P("row", "col"), P("row", None), P("row", "col"), P("row", "col")),
        check_vma=False,
    )
```

```python
import functools

import jax
import jax.numpy as jnp
from jax import lax
from jax.experimental import pallas as pl
from jax.experimental.pallas import tpu as pltpu
from jax.sharding import PartitionSpec as P

PB = 256
HB = 128
TILE = 128
BOTH = ("col", "row")
precise = lax.Precision.HIGHEST
F32 = jnp.float32


def mm(a, b, dims=((1,), (0,))):
    return lax.dot_general(a, b, (dims, ((), ())), precision=precise, preferred_element_type=F32)


def split(x):
    hi = x.astype(jnp.bfloat16)
    return hi, (x - hi.astype(F32)).astype(jnp.bfloat16)


def left(x, axis=1):
    hi, lo = split(x)
    return jnp.concatenate([hi, hi, lo], axis=axis)


def right(x, axis=1):
    hi, lo = split(x)
    return jnp.concatenate([hi, lo, hi], axis=axis)


def dot3(a, b, dims=((1,), (0,))):
    return lax.dot_general(a, b, (dims, ((), ())), preferred_element_type=F32)


def inverse_factor(a_ref, w_ref):
    n = a_ref.shape[0]
    rows = lax.broadcasted_iota(jnp.int32, (n, n), 0)
    lanes = lax.broadcasted_iota(jnp.int32, (n, n), 1)
    groups = rows.reshape(n // 8, 8, n)
    w_ref[...] = jnp.where(rows == lanes, 1.0, 0.0).astype(F32)

    def pick(x, index):
        return jnp.take_along_axis(
            x, jnp.full(x.shape, index, jnp.int32), axis=1, mode="promise_in_bounds"
        )

    def step(it, carry):
        k = it * 4
        a = a_ref[...]
        c = [pick(a, k + t).reshape(n // 8, 8, n) for t in range(4)]
        a = a.reshape(n // 8, 8, n)
        w = w_ref[...].reshape(n // 8, 8, n)
        r = [jnp.broadcast_to(a_ref[pl.ds(k + t, 1), :], (8, n)) for t in range(4)]
        v = [jnp.broadcast_to(w_ref[pl.ds(k + t, 1), :], (8, n)) for t in range(4)]
        g = [[pick(r[t], k + s) for s in range(4)] for t in range(4)]
        inv = []
        for t in range(4):
            inv.append(1.0 / g[t][t])
            for s in range(t + 1, 4):
                m = g[t][s] * inv[t]
                for u in range(s, 4):
                    g[s][u] = g[s][u] - m * g[t][u]
                r[s] = r[s] - m * r[t]
                v[s] = v[s] - m * v[t]
        for t in range(4):
            m = c[t] * inv[t]
            for s in range(t + 1, 4):
                c[s] = c[s] - m * g[t][s]
            m = jnp.where(groups >= k + 4, m, 0.0)
            a = a - m * r[t]
            w = w - m * v[t]
        a_ref[...] = a.reshape(n, n)
        w_ref[...] = w.reshape(n, n)
        for t in range(4):
            d = g[t][t]
            y = lax.rsqrt(d)
            y = y * (1.5 - 0.5 * d * y * y)
            w_ref[pl.ds(k + t, 1), :] = (v[t] * y)[:1]
        return carry

    lax.fori_loop(0, n // 4, step, 0)


def factor_kernel(d_ref, out_ref, a_ref, w1_ref, w2_ref):
    a_ref[...] = d_ref[:HB, :]
    inverse_factor(a_ref, w1_ref)
    first = w1_ref[...]
    low = mm(d_ref[HB:PB, :], first, ((1,), (1,)))
    a_ref[...] = d_ref[PB:, :] - mm(low, low, ((1,), (1,)))
    inverse_factor(a_ref, w2_ref)
    second = w2_ref[...]
    out_ref[:HB, :] = first
    out_ref[HB:PB, :] = -mm(second, mm(low, first))
    out_ref[PB:, :] = second


def inverse_of_factor(block):
    return pl.pallas_call(
        factor_kernel,
        out_shape=jax.ShapeDtypeStruct((3 * HB, HB), F32),
        scratch_shapes=[pltpu.VMEM((HB, HB), F32)] * 3,
        compiler_params=pltpu.CompilerParams(vmem_limit_bytes=8 << 20),
        cost_estimate=pl.CostEstimate(
            flops=200_000_000, transcendentals=0, bytes_accessed=80_000_000
        ),
        name="inverse_factor",
    )(block)


def two_halves(ref, base):
    stack = ref[:, base : base + 24, :].reshape(-1, HB)
    half = stack.shape[0] // 2
    return jnp.concatenate([stack[:half], stack[half:]], axis=1)


def noise_row(noise_ref, wfs):
    noise = jnp.zeros(wfs.shape, F32)
    for s in range(noise_ref.shape[0]):
        noise = jnp.where(wfs == s, noise_ref[s], noise)
    return noise


def iotas():
    shape = (PB, PB)
    return lax.broadcasted_iota(jnp.int32, shape, 0), lax.broadcasted_iota(jnp.int32, shape, 1)


def solve_kernel(
    place_ref, noise_ref, wfs_ref, own_ref, inv_ref, a_ref, t_ref,
    pan_ref, inv3_ref, pair_ref, mine_ref, a_out, t_out, sems,
):
    copies = [
        pltpu.make_async_copy(a_ref, a_out, sems.at[0]),
        pltpu.make_async_copy(t_ref, t_out, sems.at[1]),
    ]
    for copy in copies:
        copy.start()
    inv = jnp.concatenate(
        [
            jnp.concatenate([inv_ref[:HB, :], jnp.zeros((HB, HB), F32)], axis=1),
            jnp.concatenate([inv_ref[HB:PB, :], inv_ref[PB:, :]], axis=1),
        ],
        axis=0,
    )
    inv3_ref[...] = left(inv)
    inv3 = inv3_ref[...]
    pan_ref[...] = dot3(right(two_halves(own_ref, 0)), inv3, ((1,), (1,)))

    @pl.when(place_ref[0] == 0)
    def _():
        sub, lane = iotas()
        noise = noise_row(noise_ref, wfs_ref[:, :PB])
        block = two_halves(own_ref, 0)[:PB] + jnp.where(sub == lane, noise, 0.0)
        lead = dot3(right(block), inv3, ((1,), (1,)))
        pan_ref[:PB, :] = jnp.where(lane > sub, 0.0, lead)

    pair_ref[...] = left(pan_ref[...])
    mine_ref[...] = right(dot3(inv3, right(two_halves(own_ref, 24)), ((1,), (1,))), axis=0)
    for copy in copies:
        copy.wait()


def solve(place, noise_var, wfs, own, inv, covariance, targets):
    rows = covariance.shape[0]
    anywhere = pl.BlockSpec(memory_space=pl.ANY)
    far = lambda x: pltpu.with_memory_space_constraint(x, pltpu.HBM)
    return pl.pallas_call(
        solve_kernel,
        in_specs=[SMEM, SMEM, VMEM, VMEM, VMEM, anywhere, anywhere],
        out_specs=[VMEM] * 6,
        out_shape=[
            pltpu.VMEM((rows, PB), F32),
            pltpu.VMEM((PB, 3 * PB), jnp.bfloat16),
            pltpu.VMEM((rows, 3 * PB), jnp.bfloat16),
            pltpu.VMEM((3 * PB, rows), jnp.bfloat16),
            pltpu.VMEM(covariance.shape, F32),
            pltpu.VMEM(targets.shape, F32),
        ],
        scratch_shapes=[pltpu.SemaphoreType.DMA((2,))],
        compiler_params=pltpu.CompilerParams(vmem_limit_bytes=20 << 20),
        cost_estimate=pl.CostEstimate(
            flops=1_000_000_000, transcendentals=0, bytes_accessed=6_000_000
        ),
        name="solve",
    )(place, noise_var, wfs, own, inv, far(covariance), far(targets))


def update_kernel(
    place_ref, noise_ref, wfs_ref, a_ref, t_ref, own_ref, other_ref, panel_ref, inv3_ref, pair_ref,
    mine_ref, ctt_ref, upd_ref, pan_ref, rec_ref, err_ref, theirs_ref, head_ref, head3_ref,
):
    i = pl.program_id(0)
    row, col = place_ref[0], place_ref[1]
    core = lax.rem(row, 2)
    tile, width = upd_ref.shape
    half = width // 2

    @pl.when(i == 0)
    def _():
        inv3 = inv3_ref[...]
        raw = right(two_halves(other_ref, 0))
        theirs_ref[...] = right(dot3(inv3, raw, ((1,), (1,))), axis=0)
        mine = own_ref[:, 52:56, :].reshape(PB, HB)
        other = other_ref[:, 28:32, :].reshape(PB, HB)
        first = jnp.where(core == 0, mine, other)
        last = jnp.where(core == 0, other, mine)
        head = dot3(inv3, right(jnp.concatenate([first, last], axis=1), axis=0))
        head_ref[...] = head
        head3_ref[...] = right(head, axis=0)
        need = dot3(inv3, right(own_ref[:, 48:52, :].reshape(PB, HB), axis=0))
        err_ref[...] = ctt_ref[...] - dot3(left(need, axis=0), head3_ref[...], ((0,), (0,)))

    here = pl.ds(pl.multiple_of(i * tile, tile), tile)
    pair = pair_ref[here, :]
    for at, ref in ((core, mine_ref), (1 - core, theirs_ref)):
        where = pl.ds(pl.multiple_of(at * half, half), half)
        upd_ref[:, where] = a_ref[here, where] - dot3(pair, ref[...])
    pan_ref[...] = panel_ref[here, :]
    rec_ref[...] = t_ref[here, :] - dot3(pair, head3_ref[...])

    @pl.when(lax.div(row, 2) == col)
    def _():
        where = pl.ds(pl.multiple_of(core * half + i * tile, PB), PB)
        sub, lane = iotas()
        noise = noise_row(noise_ref, wfs_ref[...])
        upd_ref[:, where] = upd_ref[:, where] + jnp.where(sub == lane, noise, 0.0)

    @pl.when((row == 0) & (i == 0))
    def _():
        upd_ref[...] = jnp.zeros_like(upd_ref)
        rec_ref[...] = head_ref[...]

    @pl.when(col == 0)
    def _():
        upd_ref[:, :PB] = panel_ref[here, :]


SMEM = pl.BlockSpec(memory_space=pltpu.SMEM)
VMEM = pl.BlockSpec(memory_space=pltpu.VMEM)


def update(place, noise_var, wfs, matrix, targets, own, other, solved, ctt):
    rows, width = matrix.shape
    target_width = targets.shape[1]
    tiled = lambda n: pl.BlockSpec((PB, n), lambda i: (i, 0))
    near = lambda x: pltpu.with_memory_space_constraint(x, pltpu.VMEM)
    return pl.pallas_call(
        update_kernel,
        grid=(rows // PB,),
        in_specs=[SMEM, SMEM, pl.BlockSpec((1, PB), lambda i: (0, i))]
        + [VMEM] * 9,
        out_specs=[
            tiled(width),
            tiled(PB),
            tiled(target_width),
            pl.BlockSpec(ctt.shape, lambda i: (0, 0)),
        ],
        out_shape=[
            jax.ShapeDtypeStruct((rows, width), F32),
            jax.ShapeDtypeStruct((rows, PB), F32),
            jax.ShapeDtypeStruct((rows, target_width), F32),
            jax.ShapeDtypeStruct(ctt.shape, F32),
        ],
        scratch_shapes=[
            pltpu.VMEM((3 * PB, width // 2), jnp.bfloat16),
            pltpu.VMEM((PB, target_width), F32),
            pltpu.VMEM((3 * PB, target_width), jnp.bfloat16),
        ],
        compiler_params=pltpu.CompilerParams(vmem_limit_bytes=20 << 20),
        cost_estimate=pl.CostEstimate(
            flops=2_000_000_000, transcendentals=0, bytes_accessed=7_000_000
        ),
        name="update",
    )(
        place, noise_var, wfs, near(matrix), near(targets), near(own), near(other),
        *[near(x) for x in solved], near(ctt),
    )


def pieces_kernel(a_ref, t_ref, second_ref, out_ref):
    half = jnp.where(lax.axis_index("row") == 1, second_ref[...], t_ref[...])
    count = out_ref.shape[0] // 2
    out_ref[:count, :24, :] = a_ref[:, :HB].reshape(count, 24, HB)
    out_ref[count:, :24, :] = a_ref[:, HB:].reshape(count, 24, HB)
    half = half.reshape(2 * count, 4, HB)
    out_ref[:, 24:, :] = jnp.concatenate([half, jnp.zeros_like(half)], axis=1)


def pieces_of(covariance, targets, second):
    far = lambda x: pltpu.with_memory_space_constraint(x, pltpu.HBM)
    rows = covariance.shape[0]
    first = lambda *shape: pl.BlockSpec(shape, lambda i: (0,) * len(shape))
    return pl.pallas_call(
        pieces_kernel,
        grid=(1,),
        in_specs=[first(rows, PB), first(PB, HB), first(PB, HB)],
        out_specs=first(64, 32, HB),
        out_shape=jax.ShapeDtypeStruct((64, 32, HB), F32),
        compiler_params=pltpu.CompilerParams(vmem_limit_bytes=8 << 20),
        cost_estimate=pl.CostEstimate(flops=0, transcendentals=0, bytes_accessed=2_000_000),
        name="pieces",
    )(far(covariance), far(targets), second)


def lead_kernel(a_ref, noise_ref, out_ref):
    sub = lax.broadcasted_iota(jnp.int32, (HB, HB), 0)
    eye = sub == lax.broadcasted_iota(jnp.int32, (HB, HB), 1)
    here = (lax.axis_index("row") == 0) & (lax.axis_index("col") == 0)
    keep = lambda x: jnp.where(here, x, 0.0)
    out_ref[:HB] = keep(a_ref[:HB, :HB] + jnp.where(eye, noise_ref[:, :HB], 0.0))
    out_ref[HB:PB] = keep(a_ref[HB:, :HB])
    out_ref[PB:] = keep(a_ref[HB:, HB:] + jnp.where(eye, noise_ref[:, HB:], 0.0))


def lead_of(covariance, noise):
    first = lambda *shape: pl.BlockSpec(shape, lambda i: (0, 0))
    return pl.pallas_call(
        lead_kernel,
        grid=(1,),
        in_specs=[first(PB, PB), first(1, PB)],
        out_specs=first(3 * HB, HB),
        out_shape=jax.ShapeDtypeStruct((3 * HB, HB), F32),
        compiler_params=pltpu.CompilerParams(vmem_limit_bytes=4 << 20),
        cost_estimate=pl.CostEstimate(flops=0, transcendentals=0, bytes_accessed=500_000),
        name="lead",
    )(pltpu.with_memory_space_constraint(covariance, pltpu.HBM), noise)


def device(x, z_lo, y, z_hi, core):
    return (x * 2 + z_lo) * 16 + y * 4 + z_hi * 2 + core


def rounds_of():
    four, two = range(4), range(2)
    return (
        [[(device(0, 0, 0, 0, 0), device(k, 0, 0, 0, 0))] for k in (2, 1, 3)],
        [[(device(x, 0, 0, 0, 0), device(x, 0, k, 0, 0)) for x in four] for k in (2, 1, 3)],
        [
            [(device(x, 0, y, 0, 0), device(x, lo, y, hi, 0)) for x in four for y in four]
            for lo, hi in ((0, 1), (1, 1), (1, 0))
        ],
        [
            [
                (device(x, lo, y, hi, 0), device(x, lo, y, hi, 1))
                for x in four for y in four for lo in two for hi in two
            ]
        ],
    )


def wave(value, perms):
    return sum([lax.ppermute(value, BOTH, perm) for perm in perms], value)


def target_covariance(pos_rows, pos_cols, low, strength, scale):
    distance = (pos_rows[0][:, None] - pos_cols[0][None, :]) ** 2 + (
        pos_rows[1][:, None] - pos_cols[1][None, :]
    ) ** 2
    levels = jnp.arange(strength.shape[0], dtype=jnp.int32)
    weights = strength[:, None, None] / (1.0 + distance[None] / (scale * scale)[:, None, None])
    return jnp.sum(jnp.where(levels[:, None, None] <= low[None, None, :], weights, 0.0), axis=0)


def local(covariance, wfs_map, noise_var, targets, target_pos, strength, scale, tile_layer):
    rows, width = covariance.shape
    target_width = targets.shape[1]
    row, col = lax.axis_index("row"), lax.axis_index("col")
    groups = [[c * 16 + 2 * m + k for c in range(8) for m in range(8)] for k in range(2)]
    exchange = lambda x: lax.all_to_all(
        x, BOTH, 0, 0, axis_index_groups=groups, tiled=True
    )

    second = lax.ppermute(targets[:PB, HB:], "row", [(0, 1)])
    pieces = pieces_of(covariance, targets, second)

    kinds = jnp.arange(noise_var.shape[0], dtype=jnp.int32)[:, None]
    noise = jnp.sum(
        jnp.where(wfs_map[None, :PB] == kinds, noise_var[:, None], 0.0), axis=0, keepdims=True
    )
    lead = lead_of(covariance, noise)
    along_x, along_y, along_z, to_core = rounds_of()
    lead, _ = lax.optimization_barrier((wave(lead, along_x), pieces))
    lead = wave(lead, along_y)

    position, levels, _ = lax.optimization_barrier((target_pos, tile_layer, lead))
    start = row * TILE
    pos_rows = lax.dynamic_slice_in_dim(position, start, TILE, 1)
    pos_cols = lax.dynamic_slice_in_dim(position, col * target_width, target_width, 1)
    level_cols = lax.dynamic_slice_in_dim(levels, col * (target_width // TILE), target_width // TILE, 0)
    level_row = lax.dynamic_slice_in_dim(levels, row, 1, 0)
    low = jnp.repeat(jnp.minimum(level_row, level_cols), TILE)
    ctt = target_covariance(pos_rows, pos_cols, low, strength, scale)

    place = jnp.stack([row, col]).astype(jnp.int32)
    wfs_row, place, _ = lax.optimization_barrier((wfs_map, place, lead))
    wfs_row = wfs_row[None, :]
    lead, ctt, wfs_row, place = lax.optimization_barrier(
        (wave(lead, along_z), ctt, wfs_row, place)
    )
    held = exchange(pieces)
    held_panel = held[:8, :24]
    held_head = held.reshape(8, 8, 32, HB)[:, 0, 24:28]

    shape = lambda n: (8, 8, n, HB)
    over_m = lambda x: jnp.broadcast_to(x[None], shape(x.shape[1]))
    over_c = lambda x: jnp.broadcast_to(x[:, None], shape(x.shape[1]))
    wanted = jnp.concatenate(
        [over_m(held_panel), over_c(held_panel), over_m(held_head), over_c(held_head)], axis=2
    ).reshape(64, 56, HB)
    wanted, _ = lax.optimization_barrier((wanted, lead))
    lead, _ = lax.optimization_barrier((wave(lead, to_core), wanted))
    inv = inverse_of_factor(lead)
    own, inv = lax.optimization_barrier((exchange(wanted), inv))
    other = lax.ppermute(own[:, 24:], "row", [(i, i ^ 1) for i in range(16)])

    *solved, matrix, near_targets = solve(
        place, noise_var, wfs_row, own, inv, covariance, targets
    )
    return update(
        place, noise_var, wfs_row, matrix, near_targets, own, other, solved, ctt
    )


def solution(mesh):
    placed = (P("row", "col"), P("row"), P(), P("row", "col"), P(), P(), P(), P())
    return jax.shard_map(
        local,
        mesh=mesh,
        in_specs=placed,
        out_specs=(P("row", "col"), P("row", None), P("row", "col"), P("row", "col")),
        check_vma=False,
    )
```

```python
import functools

import jax
import jax.numpy as jnp
from jax import lax
from jax.experimental import pallas as pl
from jax.experimental.pallas import tpu as pltpu
from jax.sharding import PartitionSpec as P

PB = 256
HB = 128
TILE = 128
BOTH = ("col", "row")
precise = lax.Precision.HIGHEST
F32 = jnp.float32
SMEM = pl.BlockSpec(memory_space=pltpu.SMEM)
VMEM = pl.BlockSpec(memory_space=pltpu.VMEM)


def mm(a, b, dims=((1,), (0,))):
    return lax.dot_general(a, b, (dims, ((), ())), precision=precise, preferred_element_type=F32)


def split(x):
    hi = x.astype(jnp.bfloat16)
    return hi, (x - hi.astype(F32)).astype(jnp.bfloat16)


def left(x, axis=1):
    hi, lo = split(x)
    return jnp.concatenate([hi, hi, lo], axis=axis)


def right(x, axis=1):
    hi, lo = split(x)
    return jnp.concatenate([hi, lo, hi], axis=axis)


def dot3(a, b, dims=((1,), (0,))):
    return lax.dot_general(a, b, (dims, ((), ())), preferred_element_type=F32)


def inverse_factor(a_ref, w_ref):
    n = a_ref.shape[0]
    rows = lax.broadcasted_iota(jnp.int32, (n, n), 0)
    lanes = lax.broadcasted_iota(jnp.int32, (n, n), 1)
    groups = rows.reshape(n // 8, 8, n)
    w_ref[...] = jnp.where(rows == lanes, 1.0, 0.0).astype(F32)

    def pick(x, index):
        return jnp.take_along_axis(
            x, jnp.full(x.shape, index, jnp.int32), axis=1, mode="promise_in_bounds"
        )

    def step(it, carry):
        k = it * 4
        a = a_ref[...]
        c = [pick(a, k + t).reshape(n // 8, 8, n) for t in range(4)]
        a = a.reshape(n // 8, 8, n)
        w = w_ref[...].reshape(n // 8, 8, n)
        r = [jnp.broadcast_to(a_ref[pl.ds(k + t, 1), :], (8, n)) for t in range(4)]
        v = [jnp.broadcast_to(w_ref[pl.ds(k + t, 1), :], (8, n)) for t in range(4)]
        g = [[pick(r[t], k + s) for s in range(4)] for t in range(4)]
        inv = []
        for t in range(4):
            inv.append(1.0 / g[t][t])
            for s in range(t + 1, 4):
                m = g[t][s] * inv[t]
                for u in range(s, 4):
                    g[s][u] = g[s][u] - m * g[t][u]
                r[s] = r[s] - m * r[t]
                v[s] = v[s] - m * v[t]
        for t in range(4):
            m = c[t] * inv[t]
            for s in range(t + 1, 4):
                c[s] = c[s] - m * g[t][s]
            m = jnp.where(groups >= k + 4, m, 0.0)
            a = a - m * r[t]
            w = w - m * v[t]
        a_ref[...] = a.reshape(n, n)
        w_ref[...] = w.reshape(n, n)
        for t in range(4):
            d = g[t][t]
            y = lax.rsqrt(d)
            y = y * (1.5 - 0.5 * d * y * y)
            w_ref[pl.ds(k + t, 1), :] = (v[t] * y)[:1]
        return carry

    lax.fori_loop(0, n // 4, step, 0)


def factor_kernel(
    d_ref, big_ref, t_ref, out_ref, big_out, t_out, a_ref, w1_ref, w2_ref, sems
):
    copies = [
        pltpu.make_async_copy(big_ref, big_out, sems.at[0]),
        pltpu.make_async_copy(t_ref, t_out, sems.at[1]),
    ]
    for copy in copies:
        copy.start()
    a_ref[...] = d_ref[:HB, :]
    inverse_factor(a_ref, w1_ref)
    first = w1_ref[...]
    low = mm(d_ref[HB:PB, :], first, ((1,), (1,)))
    a_ref[...] = d_ref[PB:, :] - mm(low, low, ((1,), (1,)))
    inverse_factor(a_ref, w2_ref)
    second = w2_ref[...]
    out_ref[:HB, :] = first
    out_ref[HB:PB, :] = -mm(second, mm(low, first))
    out_ref[PB:, :] = second
    for copy in copies:
        copy.wait()


def inverse_of_factor(block, covariance, targets):
    anywhere = pl.BlockSpec(memory_space=pl.ANY)
    far = lambda x: pltpu.with_memory_space_constraint(x, pltpu.HBM)
    return pl.pallas_call(
        factor_kernel,
        in_specs=[VMEM, anywhere, anywhere],
        out_specs=[VMEM] * 3,
        out_shape=[
            pltpu.VMEM((3 * HB, HB), F32),
            pltpu.VMEM(covariance.shape, F32),
            pltpu.VMEM(targets.shape, F32),
        ],
        scratch_shapes=[pltpu.VMEM((HB, HB), F32)] * 3 + [pltpu.SemaphoreType.DMA((2,))],
        compiler_params=pltpu.CompilerParams(vmem_limit_bytes=8 << 20),
        cost_estimate=pl.CostEstimate(
            flops=200_000_000, transcendentals=0, bytes_accessed=80_000_000
        ),
        name="inverse_factor",
    )(block, far(covariance), far(targets))


def two_halves(ref, base):
    stack = ref[:, base : base + 24, :].reshape(-1, HB)
    half = stack.shape[0] // 2
    return jnp.concatenate([stack[:half], stack[half:]], axis=1)


def noise_row(noise_ref, wfs):
    noise = jnp.zeros(wfs.shape, F32)
    for s in range(noise_ref.shape[0]):
        noise = jnp.where(wfs == s, noise_ref[s], noise)
    return noise


def iotas():
    shape = (PB, PB)
    return lax.broadcasted_iota(jnp.int32, shape, 0), lax.broadcasted_iota(jnp.int32, shape, 1)


def solve_kernel(
    place_ref, noise_ref, wfs_ref, own_ref, inv_ref, pan_ref, inv3_ref, pair_ref, mine_ref
):
    inv = jnp.concatenate(
        [
            jnp.concatenate([inv_ref[:HB, :], jnp.zeros((HB, HB), F32)], axis=1),
            jnp.concatenate([inv_ref[HB:PB, :], inv_ref[PB:, :]], axis=1),
        ],
        axis=0,
    )
    inv3_ref[...] = left(inv)
    inv3 = inv3_ref[...]
    pan_ref[...] = dot3(right(two_halves(own_ref, 0)), inv3, ((1,), (1,)))

    @pl.when(place_ref[0] == 0)
    def _():
        sub, lane = iotas()
        noise = noise_row(noise_ref, wfs_ref[:, :PB])
        block = two_halves(own_ref, 0)[:PB] + jnp.where(sub == lane, noise, 0.0)
        lead = dot3(right(block), inv3, ((1,), (1,)))
        pan_ref[:PB, :] = jnp.where(lane > sub, 0.0, lead)

    pair_ref[...] = left(pan_ref[...])
    mine_ref[...] = right(dot3(inv3, right(two_halves(own_ref, 24)), ((1,), (1,))), axis=0)


def share_kernel(own_ref, out_ref):
    out_ref[...] = own_ref[:, 24:, :]


def share_of(own):
    return pl.pallas_call(
        share_kernel,
        in_specs=[VMEM],
        out_specs=VMEM,
        out_shape=pltpu.VMEM((own.shape[0], own.shape[1] - 24, HB), F32),
        compiler_params=pltpu.CompilerParams(vmem_limit_bytes=1 << 20),
        name="share",
    )(own)


def solve(place, noise_var, wfs, own, inv, rows):
    return pl.pallas_call(
        solve_kernel,
        in_specs=[SMEM, SMEM, VMEM, VMEM, VMEM],
        out_specs=[VMEM] * 4,
        out_shape=[
            pltpu.VMEM((rows, PB), F32),
            pltpu.VMEM((PB, 3 * PB), jnp.bfloat16),
            pltpu.VMEM((rows, 3 * PB), jnp.bfloat16),
            pltpu.VMEM((3 * PB, rows), jnp.bfloat16),
        ],
        compiler_params=pltpu.CompilerParams(vmem_limit_bytes=20 << 20),
        cost_estimate=pl.CostEstimate(
            flops=1_000_000_000, transcendentals=0, bytes_accessed=6_000_000
        ),
        name="solve",
    )(place, noise_var, wfs, own, inv)


def update_kernel(
    place_ref, noise_ref, wfs_ref, a_ref, t_ref, own_ref, other_ref, panel_ref, inv3_ref, pair_ref,
    mine_ref, ctt_ref, upd_ref, pan_ref, rec_ref, err_ref, theirs_ref, head_ref, head3_ref,
):
    i = pl.program_id(0)
    row, col = place_ref[0], place_ref[1]
    core = lax.rem(row, 2)
    tile, width = upd_ref.shape
    half = width // 2

    @pl.when(i == 0)
    def _():
        inv3 = inv3_ref[...]
        raw = right(two_halves(other_ref, 0))
        theirs_ref[...] = right(dot3(inv3, raw, ((1,), (1,))), axis=0)
        mine = own_ref[:, 52:56, :].reshape(PB, HB)
        other = other_ref[:, 28:32, :].reshape(PB, HB)
        first = jnp.where(core == 0, mine, other)
        last = jnp.where(core == 0, other, mine)
        head = dot3(inv3, right(jnp.concatenate([first, last], axis=1), axis=0))
        head_ref[...] = head
        head3_ref[...] = right(head, axis=0)
        need = dot3(inv3, right(own_ref[:, 48:52, :].reshape(PB, HB), axis=0))
        err_ref[...] = ctt_ref[...] - dot3(left(need, axis=0), head3_ref[...], ((0,), (0,)))

    here = pl.ds(pl.multiple_of(i * tile, tile), tile)
    pair = pair_ref[here, :]
    for at, ref in ((core, mine_ref), (1 - core, theirs_ref)):
        where = pl.ds(pl.multiple_of(at * half, half), half)
        upd_ref[:, where] = a_ref[here, where] - dot3(pair, ref[...])
    pan_ref[...] = panel_ref[here, :]
    rec_ref[...] = t_ref[here, :] - dot3(pair, head3_ref[...])

    @pl.when(lax.div(row, 2) == col)
    def _():
        where = pl.ds(pl.multiple_of(core * half + i * tile, PB), PB)
        sub, lane = iotas()
        noise = noise_row(noise_ref, wfs_ref[...])
        upd_ref[:, where] = upd_ref[:, where] + jnp.where(sub == lane, noise, 0.0)

    @pl.when((row == 0) & (i == 0))
    def _():
        upd_ref[...] = jnp.zeros_like(upd_ref)
        rec_ref[...] = head_ref[...]

    @pl.when(col == 0)
    def _():
        upd_ref[:, :PB] = panel_ref[here, :]


def update(place, noise_var, wfs, matrix, targets, own, other, solved, ctt):
    rows, width = matrix.shape
    target_width = targets.shape[1]
    tiled = lambda n: pl.BlockSpec((PB, n), lambda i: (i, 0))
    near = lambda x: pltpu.with_memory_space_constraint(x, pltpu.VMEM)
    return pl.pallas_call(
        update_kernel,
        grid=(rows // PB,),
        in_specs=[SMEM, SMEM, pl.BlockSpec((1, PB), lambda i: (0, i))]
        + [VMEM] * 9,
        out_specs=[
            tiled(width),
            tiled(PB),
            tiled(target_width),
            pl.BlockSpec(ctt.shape, lambda i: (0, 0)),
        ],
        out_shape=[
            jax.ShapeDtypeStruct((rows, width), F32),
            jax.ShapeDtypeStruct((rows, PB), F32),
            jax.ShapeDtypeStruct((rows, target_width), F32),
            jax.ShapeDtypeStruct(ctt.shape, F32),
        ],
        scratch_shapes=[
            pltpu.VMEM((3 * PB, width // 2), jnp.bfloat16),
            pltpu.VMEM((PB, target_width), F32),
            pltpu.VMEM((3 * PB, target_width), jnp.bfloat16),
        ],
        compiler_params=pltpu.CompilerParams(vmem_limit_bytes=20 << 20),
        cost_estimate=pl.CostEstimate(
            flops=2_000_000_000, transcendentals=0, bytes_accessed=7_000_000
        ),
        name="update",
    )(
        place, noise_var, wfs, near(matrix), near(targets), near(own), near(other),
        *[near(x) for x in solved], near(ctt),
    )


def pieces_kernel(a_ref, t_ref, second_ref, out_ref):
    half = jnp.where(lax.axis_index("row") == 1, second_ref[...], t_ref[...])
    count = out_ref.shape[0] // 2
    out_ref[:count, :24, :] = a_ref[:, :HB].reshape(count, 24, HB)
    out_ref[count:, :24, :] = a_ref[:, HB:].reshape(count, 24, HB)
    half = half.reshape(2 * count, 4, HB)
    out_ref[:, 24:, :] = jnp.concatenate([half, jnp.zeros_like(half)], axis=1)


def pieces_of(covariance, targets, second):
    far = lambda x: pltpu.with_memory_space_constraint(x, pltpu.HBM)
    rows = covariance.shape[0]
    first = lambda *shape: pl.BlockSpec(shape, lambda i: (0,) * len(shape))
    return pl.pallas_call(
        pieces_kernel,
        grid=(1,),
        in_specs=[first(rows, PB), first(PB, HB), first(PB, HB)],
        out_specs=first(64, 32, HB),
        out_shape=jax.ShapeDtypeStruct((64, 32, HB), F32),
        compiler_params=pltpu.CompilerParams(vmem_limit_bytes=8 << 20),
        cost_estimate=pl.CostEstimate(flops=0, transcendentals=0, bytes_accessed=2_000_000),
        name="pieces",
    )(far(covariance), far(targets), second)


def lead_kernel(a_ref, noise_ref, wfs_ref, t_ref, out_ref, half_ref):
    noise = noise_row(noise_ref, wfs_ref[...][None, :])
    sub = lax.broadcasted_iota(jnp.int32, (HB, HB), 0)
    eye = sub == lax.broadcasted_iota(jnp.int32, (HB, HB), 1)
    here = (lax.axis_index("row") == 0) & (lax.axis_index("col") == 0)
    keep = lambda x: jnp.where(here, x, 0.0)
    out_ref[:HB] = keep(a_ref[:HB, :HB] + jnp.where(eye, noise[:, :HB], 0.0))
    out_ref[HB:PB] = keep(a_ref[HB:, :HB])
    out_ref[PB:] = keep(a_ref[HB:, HB:] + jnp.where(eye, noise[:, HB:], 0.0))
    half_ref[...] = t_ref[...]


def lead_of(covariance, noise_var, wfs, targets):
    far = lambda x: pltpu.with_memory_space_constraint(x, pltpu.HBM)
    first = lambda *shape: pl.BlockSpec(shape, lambda i: (0, 0))
    return pl.pallas_call(
        lead_kernel,
        grid=(1,),
        in_specs=[
            first(PB, PB),
            SMEM,
            pl.BlockSpec((PB,), lambda i: (0,)),
            pl.BlockSpec((PB, HB), lambda i: (0, 1)),
        ],
        out_specs=[first(3 * HB, HB), first(PB, HB)],
        out_shape=[
            jax.ShapeDtypeStruct((3 * HB, HB), F32),
            jax.ShapeDtypeStruct((PB, HB), F32),
        ],
        compiler_params=pltpu.CompilerParams(vmem_limit_bytes=4 << 20),
        cost_estimate=pl.CostEstimate(flops=0, transcendentals=0, bytes_accessed=800_000),
        name="lead",
    )(far(covariance), far(noise_var), far(wfs), far(targets))


def device(x, z_lo, y, z_hi, core):
    return (x * 2 + z_lo) * 16 + y * 4 + z_hi * 2 + core


def rounds_of():
    four, two = range(4), range(2)
    return (
        [[(device(0, 0, 0, 0, 0), device(k, 0, 0, 0, 0))] for k in (2, 1, 3)],
        [[(device(x, 0, 0, 0, 0), device(x, 0, k, 0, 0)) for x in four] for k in (2, 1, 3)],
        [
            [(device(x, 0, y, 0, 0), device(x, lo, y, hi, 0)) for x in four for y in four]
            for lo, hi in ((0, 1), (1, 1), (1, 0))
        ],
        [
            [
                (device(x, lo, y, hi, 0), device(x, lo, y, hi, 1))
                for x in four for y in four for lo in two for hi in two
            ]
        ],
    )


def wave(value, perms):
    return sum([lax.ppermute(value, BOTH, perm) for perm in perms], value)


def target_covariance(pos_rows, pos_cols, low, strength, scale):
    distance = (pos_rows[0][:, None] - pos_cols[0][None, :]) ** 2 + (
        pos_rows[1][:, None] - pos_cols[1][None, :]
    ) ** 2
    levels = jnp.arange(strength.shape[0], dtype=jnp.int32)
    weights = strength[:, None, None] / (1.0 + distance[None] / (scale * scale)[:, None, None])
    return jnp.sum(jnp.where(levels[:, None, None] <= low[None, None, :], weights, 0.0), axis=0)


def local(covariance, wfs_map, noise_var, targets, target_pos, strength, scale, tile_layer):
    rows, width = covariance.shape
    target_width = targets.shape[1]
    row, col = lax.axis_index("row"), lax.axis_index("col")
    groups = [[c * 16 + 2 * m + k for c in range(8) for m in range(8)] for k in range(2)]
    exchange = lambda x: lax.all_to_all(
        x, BOTH, 0, 0, axis_index_groups=groups, tiled=True
    )

    lead, second = lead_of(covariance, noise_var, wfs_map, targets)
    second = lax.ppermute(second, "row", [(0, 1)])
    pieces = pieces_of(covariance, targets, second)

    along_x, along_y, along_z, to_core = rounds_of()
    lead, _ = lax.optimization_barrier((wave(lead, along_x), pieces))
    lead = wave(lead, along_y)

    position, levels, _ = lax.optimization_barrier((target_pos, tile_layer, lead))
    start = row * TILE
    pos_rows = lax.dynamic_slice_in_dim(position, start, TILE, 1)
    pos_cols = lax.dynamic_slice_in_dim(position, col * target_width, target_width, 1)
    level_cols = lax.dynamic_slice_in_dim(levels, col * (target_width // TILE), target_width // TILE, 0)
    level_row = lax.dynamic_slice_in_dim(levels, row, 1, 0)
    low = jnp.repeat(jnp.minimum(level_row, level_cols), TILE)
    ctt = target_covariance(pos_rows, pos_cols, low, strength, scale)

    place = jnp.stack([row, col]).astype(jnp.int32)
    wfs_row, place, _ = lax.optimization_barrier((wfs_map, place, lead))
    wfs_row = wfs_row[None, :]
    lead, ctt, wfs_row, place = lax.optimization_barrier(
        (wave(lead, along_z), ctt, wfs_row, place)
    )
    held = exchange(pieces)
    held_panel = held[:8, :24]
    held_head = held.reshape(8, 8, 32, HB)[:, 0, 24:28]

    shape = lambda n: (8, 8, n, HB)
    over_m = lambda x: jnp.broadcast_to(x[None], shape(x.shape[1]))
    over_c = lambda x: jnp.broadcast_to(x[:, None], shape(x.shape[1]))
    wanted = jnp.concatenate(
        [over_m(held_panel), over_c(held_panel), over_m(held_head), over_c(held_head)], axis=2
    ).reshape(64, 56, HB)
    wanted, _ = lax.optimization_barrier((wanted, lead))
    lead, _ = lax.optimization_barrier((wave(lead, to_core), wanted))
    inv, matrix, near_targets = inverse_of_factor(lead, covariance, targets)
    own, inv = lax.optimization_barrier((exchange(wanted), inv))
    other = lax.ppermute(share_of(own), "row", [(i, i ^ 1) for i in range(16)])

    solved = solve(place, noise_var, wfs_row, own, inv, rows)
    return update(
        place, noise_var, wfs_row, matrix, near_targets, own, other, solved, ctt
    )


def solution(mesh):
    placed = (P("row", "col"), P("row"), P(), P("row", "col"), P(), P(), P(), P())
    return jax.shard_map(
        local,
        mesh=mesh,
        in_specs=placed,
        out_specs=(P("row", "col"), P("row", None), P("row", "col"), P("row", "col")),
        check_vma=False,
    )
```

```python
import functools

import jax
import jax.numpy as jnp
from jax import lax
from jax.experimental import pallas as pl
from jax.experimental.pallas import tpu as pltpu
from jax.sharding import PartitionSpec as P

PB = 256
HB = 128
TILE = 128
BOTH = ("col", "row")
precise = lax.Precision.HIGHEST
F32 = jnp.float32
SMEM = pl.BlockSpec(memory_space=pltpu.SMEM)
VMEM = pl.BlockSpec(memory_space=pltpu.VMEM)


def mm(a, b, dims=((1,), (0,))):
    return lax.dot_general(a, b, (dims, ((), ())), precision=precise, preferred_element_type=F32)


def split(x):
    hi = x.astype(jnp.bfloat16)
    return hi, (x - hi.astype(F32)).astype(jnp.bfloat16)


def left(x, axis=1):
    hi, lo = split(x)
    return jnp.concatenate([hi, hi, lo], axis=axis)


def right(x, axis=1):
    hi, lo = split(x)
    return jnp.concatenate([hi, lo, hi], axis=axis)


def dot3(a, b, dims=((1,), (0,))):
    return lax.dot_general(a, b, (dims, ((), ())), preferred_element_type=F32)


def inverse_factor(a_ref, w_ref):
    n = a_ref.shape[0]
    rows = lax.broadcasted_iota(jnp.int32, (n, n), 0)
    lanes = lax.broadcasted_iota(jnp.int32, (n, n), 1)
    groups = rows.reshape(n // 8, 8, n)
    w_ref[...] = jnp.where(rows == lanes, 1.0, 0.0).astype(F32)

    def pick(x, index):
        return jnp.take_along_axis(
            x, jnp.full(x.shape, index, jnp.int32), axis=1, mode="promise_in_bounds"
        )

    def step(it, carry):
        k = it * 4
        a = a_ref[...]
        c = [pick(a, k + t).reshape(n // 8, 8, n) for t in range(4)]
        a = a.reshape(n // 8, 8, n)
        w = w_ref[...].reshape(n // 8, 8, n)
        r = [jnp.broadcast_to(a_ref[pl.ds(k + t, 1), :], (8, n)) for t in range(4)]
        v = [jnp.broadcast_to(w_ref[pl.ds(k + t, 1), :], (8, n)) for t in range(4)]
        g = [[pick(r[t], k + s) for s in range(4)] for t in range(4)]
        inv = []
        for t in range(4):
            inv.append(1.0 / g[t][t])
            for s in range(t + 1, 4):
                m = g[t][s] * inv[t]
                for u in range(s, 4):
                    g[s][u] = g[s][u] - m * g[t][u]
                r[s] = r[s] - m * r[t]
                v[s] = v[s] - m * v[t]
        for t in range(4):
            m = c[t] * inv[t]
            for s in range(t + 1, 4):
                c[s] = c[s] - m * g[t][s]
            m = jnp.where(groups >= k + 4, m, 0.0)
            a = a - m * r[t]
            w = w - m * v[t]
        a_ref[...] = a.reshape(n, n)
        w_ref[...] = w.reshape(n, n)
        for t in range(4):
            d = g[t][t]
            y = lax.rsqrt(d)
            y = y * (1.5 - 0.5 * d * y * y)
            w_ref[pl.ds(k + t, 1), :] = (v[t] * y)[:1]
        return carry

    lax.fori_loop(0, n // 4, step, 0)


def factor_kernel(
    d_ref, big_ref, t_ref, out_ref, big_out, t_out, a_ref, w1_ref, w2_ref, sems
):
    copies = [
        pltpu.make_async_copy(big_ref, big_out, sems.at[0]),
        pltpu.make_async_copy(t_ref, t_out, sems.at[1]),
    ]
    for copy in copies:
        copy.start()
    a_ref[...] = d_ref[:HB, :]
    inverse_factor(a_ref, w1_ref)
    first = w1_ref[...]
    low = mm(d_ref[HB:PB, :], first, ((1,), (1,)))
    a_ref[...] = d_ref[PB:, :] - mm(low, low, ((1,), (1,)))
    inverse_factor(a_ref, w2_ref)
    second = w2_ref[...]
    out_ref[:HB, :] = first
    out_ref[HB:PB, :] = -mm(second, mm(low, first))
    out_ref[PB:, :] = second
    for copy in copies:
        copy.wait()


def inverse_of_factor(block, covariance, targets):
    anywhere = pl.BlockSpec(memory_space=pl.ANY)
    far = lambda x: pltpu.with_memory_space_constraint(x, pltpu.HBM)
    return pl.pallas_call(
        factor_kernel,
        in_specs=[VMEM, anywhere, anywhere],
        out_specs=[VMEM] * 3,
        out_shape=[
            pltpu.VMEM((3 * HB, HB), F32),
            pltpu.VMEM(covariance.shape, F32),
            pltpu.VMEM(targets.shape, F32),
        ],
        scratch_shapes=[pltpu.VMEM((HB, HB), F32)] * 3 + [pltpu.SemaphoreType.DMA((2,))],
        compiler_params=pltpu.CompilerParams(vmem_limit_bytes=8 << 20),
        cost_estimate=pl.CostEstimate(
            flops=200_000_000, transcendentals=0, bytes_accessed=80_000_000
        ),
        name="inverse_factor",
    )(block, far(covariance), far(targets))


def two_halves(ref, base):
    stack = ref[:, base : base + 24, :].reshape(-1, HB)
    half = stack.shape[0] // 2
    return jnp.concatenate([stack[:half], stack[half:]], axis=1)


def noise_row(noise_ref, wfs):
    noise = jnp.zeros(wfs.shape, F32)
    for s in range(noise_ref.shape[0]):
        noise = jnp.where(wfs == s, noise_ref[s], noise)
    return noise


def iotas():
    shape = (PB, PB)
    return lax.broadcasted_iota(jnp.int32, shape, 0), lax.broadcasted_iota(jnp.int32, shape, 1)


def solve_kernel(
    place_ref, noise_ref, wfs_ref, own_ref, inv_ref, pan_ref, inv3_ref, pair_ref, mine_ref, far_ref,
    sem,
):
    inv = jnp.concatenate(
        [
            jnp.concatenate([inv_ref[:HB, :], jnp.zeros((HB, HB), F32)], axis=1),
            jnp.concatenate([inv_ref[HB:PB, :], inv_ref[PB:, :]], axis=1),
        ],
        axis=0,
    )
    inv3_ref[...] = left(inv)
    inv3 = inv3_ref[...]
    pan_ref[...] = dot3(right(two_halves(own_ref, 0)), inv3, ((1,), (1,)))

    @pl.when(place_ref[0] == 0)
    def _():
        sub, lane = iotas()
        noise = noise_row(noise_ref, wfs_ref[:, :PB])
        block = two_halves(own_ref, 0)[:PB] + jnp.where(sub == lane, noise, 0.0)
        lead = dot3(right(block), inv3, ((1,), (1,)))
        pan_ref[:PB, :] = jnp.where(lane > sub, 0.0, lead)

    copy = pltpu.make_async_copy(pan_ref, far_ref, sem)
    copy.start()
    pair_ref[...] = left(pan_ref[...])
    mine_ref[...] = right(dot3(inv3, right(two_halves(own_ref, 24)), ((1,), (1,))), axis=0)
    copy.wait()


def share_kernel(own_ref, out_ref):
    out_ref[...] = own_ref[:, 24:, :]


def share_of(own):
    return pl.pallas_call(
        share_kernel,
        in_specs=[VMEM],
        out_specs=VMEM,
        out_shape=pltpu.VMEM((own.shape[0], own.shape[1] - 24, HB), F32),
        compiler_params=pltpu.CompilerParams(vmem_limit_bytes=1 << 20),
        name="share",
    )(own)


def solve(place, noise_var, wfs, own, inv, rows):
    return pl.pallas_call(
        solve_kernel,
        in_specs=[SMEM, SMEM, VMEM, VMEM, VMEM],
        out_specs=[VMEM] * 4 + [pl.BlockSpec(memory_space=pl.ANY)],
        out_shape=[
            pltpu.VMEM((rows, PB), F32),
            pltpu.VMEM((PB, 3 * PB), jnp.bfloat16),
            pltpu.VMEM((rows, 3 * PB), jnp.bfloat16),
            pltpu.VMEM((3 * PB, rows), jnp.bfloat16),
            jax.ShapeDtypeStruct((rows, PB), F32),
        ],
        scratch_shapes=[pltpu.SemaphoreType.DMA],
        compiler_params=pltpu.CompilerParams(vmem_limit_bytes=20 << 20),
        cost_estimate=pl.CostEstimate(
            flops=1_000_000_000, transcendentals=0, bytes_accessed=6_000_000
        ),
        name="solve",
    )(place, noise_var, wfs, own, inv)


def update_kernel(
    place_ref, noise_ref, wfs_ref, a_ref, t_ref, own_ref, other_ref, panel_ref, inv3_ref, pair_ref,
    mine_ref, ctt_ref, upd_ref, rec_ref, err_ref, theirs_ref, head_ref, head3_ref,
):
    i = pl.program_id(0)
    row, col = place_ref[0], place_ref[1]
    core = lax.rem(row, 2)
    tile, width = upd_ref.shape
    half = width // 2

    @pl.when(i == 0)
    def _():
        inv3 = inv3_ref[...]
        raw = right(two_halves(other_ref, 0))
        theirs_ref[...] = right(dot3(inv3, raw, ((1,), (1,))), axis=0)
        mine = own_ref[:, 52:56, :].reshape(PB, HB)
        other = other_ref[:, 28:32, :].reshape(PB, HB)
        first = jnp.where(core == 0, mine, other)
        last = jnp.where(core == 0, other, mine)
        head = dot3(inv3, right(jnp.concatenate([first, last], axis=1), axis=0))
        head_ref[...] = head
        head3_ref[...] = right(head, axis=0)
        need = dot3(inv3, right(own_ref[:, 48:52, :].reshape(PB, HB), axis=0))
        err_ref[...] = ctt_ref[...] - dot3(left(need, axis=0), head3_ref[...], ((0,), (0,)))

    here = pl.ds(pl.multiple_of(i * tile, tile), tile)
    pair = pair_ref[here, :]
    for at, ref in ((core, mine_ref), (1 - core, theirs_ref)):
        where = pl.ds(pl.multiple_of(at * half, half), half)
        upd_ref[:, where] = a_ref[here, where] - dot3(pair, ref[...])
    rec_ref[...] = t_ref[here, :] - dot3(pair, head3_ref[...])

    @pl.when(lax.div(row, 2) == col)
    def _():
        where = pl.ds(pl.multiple_of(core * half + i * tile, PB), PB)
        sub, lane = iotas()
        noise = noise_row(noise_ref, wfs_ref[...])
        upd_ref[:, where] = upd_ref[:, where] + jnp.where(sub == lane, noise, 0.0)

    @pl.when((row == 0) & (i == 0))
    def _():
        upd_ref[...] = jnp.zeros_like(upd_ref)
        rec_ref[...] = head_ref[...]

    @pl.when(col == 0)
    def _():
        upd_ref[:, :PB] = panel_ref[here, :]


def update(place, noise_var, wfs, matrix, targets, own, other, solved, ctt):
    rows, width = matrix.shape
    target_width = targets.shape[1]
    tiled = lambda n: pl.BlockSpec((PB, n), lambda i: (i, 0))
    near = lambda x: pltpu.with_memory_space_constraint(x, pltpu.VMEM)
    return pl.pallas_call(
        update_kernel,
        grid=(rows // PB,),
        in_specs=[SMEM, SMEM, pl.BlockSpec((1, PB), lambda i: (0, i))]
        + [VMEM] * 9,
        out_specs=[
            tiled(width),
            tiled(target_width),
            pl.BlockSpec(ctt.shape, lambda i: (0, 0)),
        ],
        out_shape=[
            jax.ShapeDtypeStruct((rows, width), F32),
            jax.ShapeDtypeStruct((rows, target_width), F32),
            jax.ShapeDtypeStruct(ctt.shape, F32),
        ],
        scratch_shapes=[
            pltpu.VMEM((3 * PB, width // 2), jnp.bfloat16),
            pltpu.VMEM((PB, target_width), F32),
            pltpu.VMEM((3 * PB, target_width), jnp.bfloat16),
        ],
        compiler_params=pltpu.CompilerParams(vmem_limit_bytes=20 << 20),
        cost_estimate=pl.CostEstimate(
            flops=2_000_000_000, transcendentals=0, bytes_accessed=7_000_000
        ),
        name="update",
    )(
        place, noise_var, wfs, near(matrix), near(targets), near(own), near(other),
        *[near(x) for x in solved], near(ctt),
    )


def pieces_kernel(a_ref, t_ref, second_ref, out_ref):
    count = out_ref.shape[0]
    half = jnp.where(lax.axis_index("row") == 1, second_ref[...], t_ref[...])
    half = half.reshape(count, 4, HB)
    out_ref[:, :24, :] = a_ref[...].reshape(count, 24, HB)
    out_ref[:, 24:, :] = jnp.concatenate([half, jnp.zeros_like(half)], axis=1)


def pieces_of(covariance, targets, second):
    far = lambda x: pltpu.with_memory_space_constraint(x, pltpu.HBM)
    rows = covariance.shape[0]
    part = pl.BlockSpec((HB, HB), lambda i: (i, 0))
    return pl.pallas_call(
        pieces_kernel,
        grid=(2,),
        in_specs=[pl.BlockSpec((rows, HB), lambda i: (0, i)), part, part],
        out_specs=pl.BlockSpec((32, 32, HB), lambda i: (i, 0, 0)),
        out_shape=jax.ShapeDtypeStruct((64, 32, HB), F32),
        compiler_params=pltpu.CompilerParams(vmem_limit_bytes=8 << 20),
        cost_estimate=pl.CostEstimate(flops=0, transcendentals=0, bytes_accessed=2_000_000),
        name="pieces",
    )(far(covariance), far(targets), second)


def lead_kernel(a_ref, noise_ref, wfs_ref, t_ref, out_ref, half_ref):
    noise = noise_row(noise_ref, wfs_ref[...][None, :])
    sub = lax.broadcasted_iota(jnp.int32, (HB, HB), 0)
    eye = sub == lax.broadcasted_iota(jnp.int32, (HB, HB), 1)
    here = (lax.axis_index("row") == 0) & (lax.axis_index("col") == 0)
    keep = lambda x: jnp.where(here, x, 0.0)
    out_ref[:HB] = keep(a_ref[:HB, :HB] + jnp.where(eye, noise[:, :HB], 0.0))
    out_ref[HB:PB] = keep(a_ref[HB:, :HB])
    out_ref[PB:] = keep(a_ref[HB:, HB:] + jnp.where(eye, noise[:, HB:], 0.0))
    half_ref[...] = t_ref[...]


def lead_of(covariance, noise_var, wfs, targets):
    far = lambda x: pltpu.with_memory_space_constraint(x, pltpu.HBM)
    first = lambda *shape: pl.BlockSpec(shape, lambda i: (0, 0))
    return pl.pallas_call(
        lead_kernel,
        grid=(1,),
        in_specs=[
            first(PB, PB),
            SMEM,
            pl.BlockSpec((PB,), lambda i: (0,)),
            pl.BlockSpec((PB, HB), lambda i: (0, 1)),
        ],
        out_specs=[first(3 * HB, HB), first(PB, HB)],
        out_shape=[
            jax.ShapeDtypeStruct((3 * HB, HB), F32),
            jax.ShapeDtypeStruct((PB, HB), F32),
        ],
        compiler_params=pltpu.CompilerParams(vmem_limit_bytes=4 << 20),
        cost_estimate=pl.CostEstimate(flops=0, transcendentals=0, bytes_accessed=800_000),
        name="lead",
    )(far(covariance), far(noise_var), far(wfs), far(targets))


def device(x, z_lo, y, z_hi, core):
    return (x * 2 + z_lo) * 16 + y * 4 + z_hi * 2 + core


def rounds_of():
    four, two = range(4), range(2)
    return (
        [[(device(0, 0, 0, 0, 0), device(k, 0, 0, 0, 0))] for k in (2, 1, 3)],
        [[(device(x, 0, 0, 0, 0), device(x, 0, k, 0, 0)) for x in four] for k in (2, 1, 3)],
        [
            [(device(x, 0, y, 0, 0), device(x, lo, y, hi, 0)) for x in four for y in four]
            for lo, hi in ((0, 1), (1, 1), (1, 0))
        ],
        [
            [
                (device(x, lo, y, hi, 0), device(x, lo, y, hi, 1))
                for x in four for y in four for lo in two for hi in two
            ]
        ],
    )


def wave(value, perms):
    return sum([lax.ppermute(value, BOTH, perm) for perm in perms], value)


def target_covariance(pos_rows, pos_cols, low, strength, scale):
    distance = (pos_rows[0][:, None] - pos_cols[0][None, :]) ** 2 + (
        pos_rows[1][:, None] - pos_cols[1][None, :]
    ) ** 2
    levels = jnp.arange(strength.shape[0], dtype=jnp.int32)
    weights = strength[:, None, None] / (1.0 + distance[None] / (scale * scale)[:, None, None])
    return jnp.sum(jnp.where(levels[:, None, None] <= low[None, None, :], weights, 0.0), axis=0)


def local(covariance, wfs_map, noise_var, targets, target_pos, strength, scale, tile_layer):
    rows, width = covariance.shape
    target_width = targets.shape[1]
    row, col = lax.axis_index("row"), lax.axis_index("col")
    groups = [[c * 16 + 2 * m + k for c in range(8) for m in range(8)] for k in range(2)]
    exchange = lambda x: lax.all_to_all(
        x, BOTH, 0, 0, axis_index_groups=groups, tiled=True
    )

    lead, second = lead_of(covariance, noise_var, wfs_map, targets)
    second = lax.ppermute(second, "row", [(0, 1)])
    pieces = pieces_of(covariance, targets, second)

    along_x, along_y, along_z, to_core = rounds_of()
    lead, _ = lax.optimization_barrier((wave(lead, along_x), pieces))
    lead = wave(lead, along_y)

    position, levels, _ = lax.optimization_barrier((target_pos, tile_layer, lead))
    start = row * TILE
    pos_rows = lax.dynamic_slice_in_dim(position, start, TILE, 1)
    pos_cols = lax.dynamic_slice_in_dim(position, col * target_width, target_width, 1)
    level_cols = lax.dynamic_slice_in_dim(levels, col * (target_width // TILE), target_width // TILE, 0)
    level_row = lax.dynamic_slice_in_dim(levels, row, 1, 0)
    low = jnp.repeat(jnp.minimum(level_row, level_cols), TILE)
    ctt = target_covariance(pos_rows, pos_cols, low, strength, scale)

    place = jnp.stack([row, col]).astype(jnp.int32)
    wfs_row, place, _ = lax.optimization_barrier((wfs_map, place, lead))
    wfs_row = wfs_row[None, :]
    lead, ctt, wfs_row, place = lax.optimization_barrier(
        (wave(lead, along_z), ctt, wfs_row, place)
    )
    held = exchange(pieces)
    held_panel = held[:8, :24]
    held_head = held.reshape(8, 8, 32, HB)[:, 0, 24:28]

    shape = lambda n: (8, 8, n, HB)
    over_m = lambda x: jnp.broadcast_to(x[None], shape(x.shape[1]))
    over_c = lambda x: jnp.broadcast_to(x[:, None], shape(x.shape[1]))
    wanted = jnp.concatenate(
        [over_m(held_panel), over_c(held_panel), over_m(held_head), over_c(held_head)], axis=2
    ).reshape(64, 56, HB)
    wanted, _ = lax.optimization_barrier((wanted, lead))
    lead, _ = lax.optimization_barrier((wave(lead, to_core), wanted))
    inv, matrix, near_targets = inverse_of_factor(lead, covariance, targets)
    own, inv = lax.optimization_barrier((exchange(wanted), inv))
    other = lax.ppermute(share_of(own), "row", [(i, i ^ 1) for i in range(16)])

    *solved, panel = solve(place, noise_var, wfs_row, own, inv, rows)
    updated, reconstructor, error = update(
        place, noise_var, wfs_row, matrix, near_targets, own, other, solved, ctt
    )
    return updated, panel, reconstructor, error


def solution(mesh):
    placed = (P("row", "col"), P("row"), P(), P("row", "col"), P(), P(), P(), P())
    return jax.shard_map(
        local,
        mesh=mesh,
        in_specs=placed,
        out_specs=(P("row", "col"), P("row", None), P("row", "col"), P("row", "col")),
        check_vma=False,
    )
```

```python
import functools

import jax
import jax.numpy as jnp
from jax import lax
from jax.experimental import pallas as pl
from jax.experimental.pallas import tpu as pltpu
from jax.sharding import PartitionSpec as P

PB = 256
HB = 128
TILE = 128
BOTH = ("col", "row")
precise = lax.Precision.HIGHEST
F32 = jnp.float32
SMEM = pl.BlockSpec(memory_space=pltpu.SMEM)
VMEM = pl.BlockSpec(memory_space=pltpu.VMEM)


def mm(a, b, dims=((1,), (0,))):
    return lax.dot_general(a, b, (dims, ((), ())), precision=precise, preferred_element_type=F32)


def split(x):
    hi = x.astype(jnp.bfloat16)
    return hi, (x - hi.astype(F32)).astype(jnp.bfloat16)


def left(x, axis=1):
    hi, lo = split(x)
    return jnp.concatenate([hi, hi, lo], axis=axis)


def right(x, axis=1):
    hi, lo = split(x)
    return jnp.concatenate([hi, lo, hi], axis=axis)


def dot3(a, b, dims=((1,), (0,))):
    return lax.dot_general(a, b, (dims, ((), ())), preferred_element_type=F32)


def inverse_factor(a_ref, w_ref):
    n = a_ref.shape[0]
    rows = lax.broadcasted_iota(jnp.int32, (n, n), 0)
    lanes = lax.broadcasted_iota(jnp.int32, (n, n), 1)
    groups = rows.reshape(n // 8, 8, n)
    w_ref[...] = jnp.where(rows == lanes, 1.0, 0.0).astype(F32)

    def pick(x, index):
        return jnp.take_along_axis(
            x, jnp.full(x.shape, index, jnp.int32), axis=1, mode="promise_in_bounds"
        )

    def step(it, carry):
        k = it * 4
        a = a_ref[...]
        c = [pick(a, k + t).reshape(n // 8, 8, n) for t in range(4)]
        a = a.reshape(n // 8, 8, n)
        w = w_ref[...].reshape(n // 8, 8, n)
        r = [jnp.broadcast_to(a_ref[pl.ds(k + t, 1), :], (8, n)) for t in range(4)]
        v = [jnp.broadcast_to(w_ref[pl.ds(k + t, 1), :], (8, n)) for t in range(4)]
        g = [[pick(r[t], k + s) for s in range(4)] for t in range(4)]
        inv = []
        for t in range(4):
            inv.append(1.0 / g[t][t])
            for s in range(t + 1, 4):
                m = g[t][s] * inv[t]
                for u in range(s, 4):
                    g[s][u] = g[s][u] - m * g[t][u]
                r[s] = r[s] - m * r[t]
                v[s] = v[s] - m * v[t]
        for t in range(4):
            m = c[t] * inv[t]
            for s in range(t + 1, 4):
                c[s] = c[s] - m * g[t][s]
            m = jnp.where(groups >= k + 4, m, 0.0)
            a = a - m * r[t]
            w = w - m * v[t]
        a_ref[...] = a.reshape(n, n)
        w_ref[...] = w.reshape(n, n)
        for t in range(4):
            d = g[t][t]
            y = lax.rsqrt(d)
            y = y * (1.5 - 0.5 * d * y * y)
            w_ref[pl.ds(k + t, 1), :] = (v[t] * y)[:1]
        return carry

    lax.fori_loop(0, n // 4, step, 0)


def factor_kernel(
    d_ref, big_ref, t_ref, out_ref, big_out, t_out, a_ref, w1_ref, w2_ref, sems
):
    copies = [
        pltpu.make_async_copy(big_ref, big_out, sems.at[0]),
        pltpu.make_async_copy(t_ref, t_out, sems.at[1]),
    ]
    for copy in copies:
        copy.start()
    a_ref[...] = d_ref[:HB, :]
    inverse_factor(a_ref, w1_ref)
    first = w1_ref[...]
    low = mm(d_ref[HB:PB, :], first, ((1,), (1,)))
    a_ref[...] = d_ref[PB:, :] - mm(low, low, ((1,), (1,)))
    inverse_factor(a_ref, w2_ref)
    second = w2_ref[...]
    out_ref[:HB, :] = first
    out_ref[HB:PB, :] = -mm(second, mm(low, first))
    out_ref[PB:, :] = second
    for copy in copies:
        copy.wait()


def inverse_of_factor(block, covariance, targets):
    anywhere = pl.BlockSpec(memory_space=pl.ANY)
    far = lambda x: pltpu.with_memory_space_constraint(x, pltpu.HBM)
    return pl.pallas_call(
        factor_kernel,
        in_specs=[VMEM, anywhere, anywhere],
        out_specs=[VMEM] * 3,
        out_shape=[
            pltpu.VMEM((3 * HB, HB), F32),
            pltpu.VMEM(covariance.shape, F32),
            pltpu.VMEM(targets.shape, F32),
        ],
        scratch_shapes=[pltpu.VMEM((HB, HB), F32)] * 3 + [pltpu.SemaphoreType.DMA((2,))],
        compiler_params=pltpu.CompilerParams(vmem_limit_bytes=8 << 20),
        cost_estimate=pl.CostEstimate(
            flops=200_000_000, transcendentals=0, bytes_accessed=80_000_000
        ),
        name="inverse_factor",
    )(block, far(covariance), far(targets))


def two_halves(ref, base):
    stack = ref[:, base : base + 24, :].reshape(-1, HB)
    half = stack.shape[0] // 2
    return jnp.concatenate([stack[:half], stack[half:]], axis=1)


def noise_row(noise_ref, wfs):
    noise = jnp.zeros(wfs.shape, F32)
    for s in range(noise_ref.shape[0]):
        noise = jnp.where(wfs == s, noise_ref[s], noise)
    return noise


def iotas():
    shape = (PB, PB)
    return lax.broadcasted_iota(jnp.int32, shape, 0), lax.broadcasted_iota(jnp.int32, shape, 1)


def solve_kernel(
    place_ref, noise_ref, wfs_ref, own_ref, inv_ref, pan_ref, inv3_ref, pair_ref, mine_ref, far_ref,
    sem,
):
    inv = jnp.concatenate(
        [
            jnp.concatenate([inv_ref[:HB, :], jnp.zeros((HB, HB), F32)], axis=1),
            jnp.concatenate([inv_ref[HB:PB, :], inv_ref[PB:, :]], axis=1),
        ],
        axis=0,
    )
    inv3_ref[...] = left(inv)
    inv3 = inv3_ref[...]
    pan_ref[...] = dot3(right(two_halves(own_ref, 0)), inv3, ((1,), (1,)))

    @pl.when(place_ref[0] == 0)
    def _():
        sub, lane = iotas()
        noise = noise_row(noise_ref, wfs_ref[:, :PB])
        block = two_halves(own_ref, 0)[:PB] + jnp.where(sub == lane, noise, 0.0)
        lead = dot3(right(block), inv3, ((1,), (1,)))
        pan_ref[:PB, :] = jnp.where(lane > sub, 0.0, lead)

    copy = pltpu.make_async_copy(pan_ref, far_ref, sem)
    copy.start()
    pair_ref[...] = left(pan_ref[...])
    mine_ref[...] = right(dot3(inv3, right(two_halves(own_ref, 24)), ((1,), (1,))), axis=0)
    copy.wait()


def share_kernel(own_ref, out_ref):
    out_ref[...] = own_ref[:, 24:, :]


def share_of(own):
    return pl.pallas_call(
        share_kernel,
        in_specs=[VMEM],
        out_specs=VMEM,
        out_shape=pltpu.VMEM((own.shape[0], own.shape[1] - 24, HB), F32),
        compiler_params=pltpu.CompilerParams(vmem_limit_bytes=1 << 20),
        name="share",
    )(own)


def solve(place, noise_var, wfs, own, inv, rows):
    return pl.pallas_call(
        solve_kernel,
        in_specs=[SMEM, SMEM, VMEM, VMEM, VMEM],
        out_specs=[VMEM] * 4 + [pl.BlockSpec(memory_space=pl.ANY)],
        out_shape=[
            pltpu.VMEM((rows, PB), F32),
            pltpu.VMEM((PB, 3 * PB), jnp.bfloat16),
            pltpu.VMEM((rows, 3 * PB), jnp.bfloat16),
            pltpu.VMEM((3 * PB, rows), jnp.bfloat16),
            jax.ShapeDtypeStruct((rows, PB), F32),
        ],
        scratch_shapes=[pltpu.SemaphoreType.DMA],
        compiler_params=pltpu.CompilerParams(vmem_limit_bytes=20 << 20),
        cost_estimate=pl.CostEstimate(
            flops=1_000_000_000, transcendentals=0, bytes_accessed=6_000_000
        ),
        name="solve",
    )(place, noise_var, wfs, own, inv)


def update_kernel(
    place_ref, noise_ref, wfs_ref, a_ref, t_ref, own_ref, other_ref, panel_ref, inv3_ref, pair_ref,
    mine_ref, ctt_ref, upd_ref, rec_ref, err_ref, theirs_ref, head_ref, head3_ref,
):
    i = pl.program_id(0)
    row, col = place_ref[0], place_ref[1]
    core = lax.rem(row, 2)
    tile, width = upd_ref.shape
    half = width // 2

    @pl.when(i == 0)
    def _():
        inv3 = inv3_ref[...]
        raw = right(two_halves(other_ref, 0))
        theirs_ref[...] = right(dot3(inv3, raw, ((1,), (1,))), axis=0)
        mine = own_ref[:, 52:56, :].reshape(PB, HB)
        other = other_ref[:, 28:32, :].reshape(PB, HB)
        first = jnp.where(core == 0, mine, other)
        last = jnp.where(core == 0, other, mine)
        head = dot3(inv3, right(jnp.concatenate([first, last], axis=1), axis=0))
        head_ref[...] = head
        head3_ref[...] = right(head, axis=0)
        need = dot3(inv3, right(own_ref[:, 48:52, :].reshape(PB, HB), axis=0))
        err_ref[...] = ctt_ref[...] - dot3(left(need, axis=0), head3_ref[...], ((0,), (0,)))

    here = pl.ds(pl.multiple_of(i * tile, tile), tile)
    pair = pair_ref[here, :]
    for at, ref in ((core, mine_ref), (1 - core, theirs_ref)):
        where = pl.ds(pl.multiple_of(at * half, half), half)
        upd_ref[:, where] = a_ref[here, where] - dot3(pair, ref[...])
    rec_ref[...] = t_ref[here, :] - dot3(pair, head3_ref[...])

    @pl.when(lax.div(row, 2) == col)
    def _():
        where = pl.ds(pl.multiple_of(core * half + i * tile, PB), PB)
        sub, lane = iotas()
        noise = noise_row(noise_ref, wfs_ref[...])
        upd_ref[:, where] = upd_ref[:, where] + jnp.where(sub == lane, noise, 0.0)

    @pl.when((row == 0) & (i == 0))
    def _():
        upd_ref[...] = jnp.zeros_like(upd_ref)
        rec_ref[...] = head_ref[...]

    @pl.when(col == 0)
    def _():
        upd_ref[:, :PB] = panel_ref[here, :]


def update(place, noise_var, wfs, matrix, targets, own, other, solved, ctt):
    rows, width = matrix.shape
    target_width = targets.shape[1]
    tiled = lambda n: pl.BlockSpec((PB, n), lambda i: (i, 0))
    near = lambda x: pltpu.with_memory_space_constraint(x, pltpu.VMEM)
    return pl.pallas_call(
        update_kernel,
        grid=(rows // PB,),
        in_specs=[SMEM, SMEM, pl.BlockSpec((1, PB), lambda i: (0, i))]
        + [VMEM] * 9,
        out_specs=[
            tiled(width),
            tiled(target_width),
            pl.BlockSpec(ctt.shape, lambda i: (0, 0)),
        ],
        out_shape=[
            jax.ShapeDtypeStruct((rows, width), F32),
            jax.ShapeDtypeStruct((rows, target_width), F32),
            jax.ShapeDtypeStruct(ctt.shape, F32),
        ],
        scratch_shapes=[
            pltpu.VMEM((3 * PB, width // 2), jnp.bfloat16),
            pltpu.VMEM((PB, target_width), F32),
            pltpu.VMEM((3 * PB, target_width), jnp.bfloat16),
        ],
        compiler_params=pltpu.CompilerParams(vmem_limit_bytes=20 << 20),
        cost_estimate=pl.CostEstimate(
            flops=2_000_000_000, transcendentals=0, bytes_accessed=7_000_000
        ),
        name="update",
    )(
        place, noise_var, wfs, near(matrix), near(targets), near(own), near(other),
        *[near(x) for x in solved], near(ctt),
    )


def pieces_kernel(a_ref, t_ref, second_ref, out_ref):
    count = out_ref.shape[0]
    half = jnp.where(lax.axis_index("row") == 1, second_ref[...], t_ref[...])
    half = half.reshape(count, 4, HB)
    out_ref[:, :24, :] = a_ref[...].reshape(count, 24, HB)
    out_ref[:, 24:, :] = jnp.concatenate([half, jnp.zeros_like(half)], axis=1)


def pieces_of(covariance, targets, second):
    far = lambda x: pltpu.with_memory_space_constraint(x, pltpu.HBM)
    rows = covariance.shape[0]
    part = pl.BlockSpec((HB, HB), lambda i: (i, 0))
    return pl.pallas_call(
        pieces_kernel,
        grid=(2,),
        in_specs=[pl.BlockSpec((rows, HB), lambda i: (0, i)), part, part],
        out_specs=pl.BlockSpec((32, 32, HB), lambda i: (i, 0, 0)),
        out_shape=jax.ShapeDtypeStruct((64, 32, HB), F32),
        compiler_params=pltpu.CompilerParams(vmem_limit_bytes=8 << 20),
        cost_estimate=pl.CostEstimate(flops=0, transcendentals=0, bytes_accessed=2_000_000),
        name="pieces",
    )(far(covariance), far(targets), second)


def lead_kernel(a_ref, noise_ref, wfs_ref, t_ref, out_ref, half_ref):
    noise = noise_row(noise_ref, wfs_ref[...][None, :])
    sub = lax.broadcasted_iota(jnp.int32, (HB, HB), 0)
    eye = sub == lax.broadcasted_iota(jnp.int32, (HB, HB), 1)
    here = (lax.axis_index("row") == 0) & (lax.axis_index("col") == 0)
    keep = lambda x: jnp.where(here, x, 0.0)
    out_ref[:HB] = keep(a_ref[:HB, :HB] + jnp.where(eye, noise[:, :HB], 0.0))
    out_ref[HB:PB] = keep(a_ref[HB:, :HB])
    out_ref[PB:] = keep(a_ref[HB:, HB:] + jnp.where(eye, noise[:, HB:], 0.0))
    half_ref[...] = t_ref[...]


def lead_of(covariance, noise_var, wfs, targets):
    far = lambda x: pltpu.with_memory_space_constraint(x, pltpu.HBM)
    first = lambda *shape: pl.BlockSpec(shape, lambda i: (0, 0))
    return pl.pallas_call(
        lead_kernel,
        grid=(1,),
        in_specs=[
            first(PB, PB),
            SMEM,
            pl.BlockSpec((PB,), lambda i: (0,)),
            pl.BlockSpec((PB, HB), lambda i: (0, 1)),
        ],
        out_specs=[first(3 * HB, HB), first(PB, HB)],
        out_shape=[
            jax.ShapeDtypeStruct((3 * HB, HB), F32),
            jax.ShapeDtypeStruct((PB, HB), F32),
        ],
        compiler_params=pltpu.CompilerParams(vmem_limit_bytes=4 << 20),
        cost_estimate=pl.CostEstimate(flops=0, transcendentals=0, bytes_accessed=800_000),
        name="lead",
    )(far(covariance), far(noise_var), far(wfs), far(targets))


def device(x, z_lo, y, z_hi, core):
    return (x * 2 + z_lo) * 16 + y * 4 + z_hi * 2 + core


def rounds_of():
    four, two = range(4), range(2)
    return (
        [[(device(0, 0, 0, 0, 0), device(k, 0, 0, 0, 0))] for k in (1, 3, 2)],
        [[(device(x, 0, 0, 0, 0), device(x, 0, k, 0, 0)) for x in four] for k in (1, 3, 2)],
        [
            [(device(x, 0, y, 0, 0), device(x, lo, y, hi, 0)) for x in four for y in four]
            for lo, hi in ((0, 1), (1, 1), (1, 0))
        ],
        [
            [
                (device(x, lo, y, hi, 0), device(x, lo, y, hi, 1))
                for x in four for y in four for lo in two for hi in two
            ]
        ],
    )


def wave(value, perms):
    return sum([lax.ppermute(value, BOTH, perm) for perm in perms], value)


def target_covariance(pos_rows, pos_cols, low, strength, scale):
    distance = (pos_rows[0][:, None] - pos_cols[0][None, :]) ** 2 + (
        pos_rows[1][:, None] - pos_cols[1][None, :]
    ) ** 2
    levels = jnp.arange(strength.shape[0], dtype=jnp.int32)
    weights = strength[:, None, None] / (1.0 + distance[None] / (scale * scale)[:, None, None])
    return jnp.sum(jnp.where(levels[:, None, None] <= low[None, None, :], weights, 0.0), axis=0)


def local(covariance, wfs_map, noise_var, targets, target_pos, strength, scale, tile_layer):
    rows, width = covariance.shape
    target_width = targets.shape[1]
    row, col = lax.axis_index("row"), lax.axis_index("col")
    groups = [[c * 16 + 2 * m + k for c in range(8) for m in range(8)] for k in range(2)]
    exchange = lambda x: lax.all_to_all(
        x, BOTH, 0, 0, axis_index_groups=groups, tiled=True
    )

    lead, second = lead_of(covariance, noise_var, wfs_map, targets)
    second = lax.ppermute(second, "row", [(0, 1)])
    pieces = pieces_of(covariance, targets, second)

    along_x, along_y, along_z, to_core = rounds_of()
    lead, _ = lax.optimization_barrier((wave(lead, along_x), pieces))
    lead = wave(lead, along_y)

    position, levels, _ = lax.optimization_barrier((target_pos, tile_layer, lead))
    start = row * TILE
    pos_rows = lax.dynamic_slice_in_dim(position, start, TILE, 1)
    pos_cols = lax.dynamic_slice_in_dim(position, col * target_width, target_width, 1)
    level_cols = lax.dynamic_slice_in_dim(levels, col * (target_width // TILE), target_width // TILE, 0)
    level_row = lax.dynamic_slice_in_dim(levels, row, 1, 0)
    low = jnp.repeat(jnp.minimum(level_row, level_cols), TILE)
    ctt = target_covariance(pos_rows, pos_cols, low, strength, scale)

    place = jnp.stack([row, col]).astype(jnp.int32)
    wfs_row, place, _ = lax.optimization_barrier((wfs_map, place, lead))
    wfs_row = wfs_row[None, :]
    lead, ctt, wfs_row, place = lax.optimization_barrier(
        (wave(lead, along_z), ctt, wfs_row, place)
    )
    held = exchange(pieces)
    held_panel = held[:8, :24]
    held_head = held.reshape(8, 8, 32, HB)[:, 0, 24:28]

    shape = lambda n: (8, 8, n, HB)
    over_m = lambda x: jnp.broadcast_to(x[None], shape(x.shape[1]))
    over_c = lambda x: jnp.broadcast_to(x[:, None], shape(x.shape[1]))
    wanted = jnp.concatenate(
        [over_m(held_panel), over_c(held_panel), over_m(held_head), over_c(held_head)], axis=2
    ).reshape(64, 56, HB)
    wanted, _ = lax.optimization_barrier((wanted, lead))
    lead, _ = lax.optimization_barrier((wave(lead, to_core), wanted))
    inv, matrix, near_targets = inverse_of_factor(lead, covariance, targets)
    own, inv = lax.optimization_barrier((exchange(wanted), inv))
    other = lax.ppermute(share_of(own), "row", [(i, i ^ 1) for i in range(16)])

    *solved, panel = solve(place, noise_var, wfs_row, own, inv, rows)
    updated, reconstructor, error = update(
        place, noise_var, wfs_row, matrix, near_targets, own, other, solved, ctt
    )
    return updated, panel, reconstructor, error


def solution(mesh):
    placed = (P("row", "col"), P("row"), P(), P("row", "col"), P(), P(), P(), P())
    return jax.shard_map(
        local,
        mesh=mesh,
        in_specs=placed,
        out_specs=(P("row", "col"), P("row", None), P("row", "col"), P("row", "col")),
        check_vma=False,
    )
```
